128 devices in a mesh: seq: 16 (over x, z_hi, core), chan: 8 (over y, z_lo).
Axes of the slice: x: 4, y: 4, z: 4 (z_hi: 2, z_lo: 2; z = z_hi * 2 + z_lo), core: 2. Of those that a mesh axis runs over, the one named last changes fastest.
Arguments:
- hidden: bfloat16 [8192, 4096], P('seq', 'chan'), may hold values from -6 to 6
- norm_gain: float32 [2048], replicated, may hold values from 0.25 to 1.75
- w_values: bfloat16 [2048, 4096], P(None, 'chan'), may hold values from -0.125 to 0.125
- w_gates: bfloat16 [2048, 4096], P(None, 'chan'), may hold values from -0.125 to 0.125
- w_control: bfloat16 [2048, 320], replicated, may hold values from -0.046875 to 0.046875
- dt_bias: float32 [64], replicated, may hold values from -1 to 1
- decay_total: float32 [64], replicated, may hold values from 0 to 274
- skip_gain: float32 [64], replicated, may hold values from 0.5 to 2
- gate_gain: float32 [4096], P('chan'), may hold values from 0.25 to 1.75
- w_out: bfloat16 [4096, 2048], P('chan'), may hold values from -0.125 to 0.125
- doc_starts: int32 [4], replicated, may hold values from 0 to 6656, as said below
Outputs:
- layer_out: bfloat16 [8192, 4096], P('seq', 'chan')
The draws below stay inside these ranges and needn't reach their ends.
Inputs may be any that keep to these rules, and one draw needn't show every extreme that they name: doc_starts[0] is 0 and the offsets rise strictly; document k runs from doc_starts[k] up to the next offset or the window's end.
All inputs are finite; a program needn't handle non-finite values.
Results may differ from the reference program's by a relative error of at most 0.013.
Values may be sent and summed in bfloat16 or wider, within the bound.
A program may use at most 128 MiB of HBM per device.

```python
import math
import jax
import jax.numpy as jnp
from jax import lax

D = 4096
HALF = 2048
INNER = 4096
HEAD_DIM = 64
STATE = 128
STRETCH = 256
HEADS = 64
SEQ_LEN = 8192
DOCS = 4


def draw_decay_total(key, part):
    key_slow, key_fast, key_pick = jax.random.split(jax.random.fold_in(key, 17), 3)
    slow_rates = jnp.exp(jax.random.uniform(key_slow, (HEADS,), jnp.float32, math.log(0.05), math.log(2.0)))
    fast_rates = jnp.exp(jax.random.uniform(key_fast, (HEADS,), jnp.float32, math.log(SEQ_LEN / 50.0), math.log(SEQ_LEN / 30.0)))
    share_slow = 0.5
    chosen = jax.random.uniform(key_pick, (HEADS,), jnp.float32) < share_slow
    return jnp.where(chosen, slow_rates, fast_rates).astype(jnp.float32)


def draw_doc_starts(key, part):
    doc_span = SEQ_LEN // DOCS
    jitter = SEQ_LEN // (4 * DOCS)
    offsets = jax.random.randint(jax.random.fold_in(key, 29), (DOCS,), -jitter, jitter + 1)
    doc_index = jnp.arange(DOCS, dtype=jnp.int32)
    offsets = jnp.where(doc_index == DOCS - 1, jitter, offsets)
    return jnp.where(doc_index == 0, 0, doc_index * doc_span + offsets).astype(jnp.int32)


def spiked(entries, own_key, source, target, blocks, factor):
    def block_of(axis_at):
        return (jnp.arange(entries.shape[axis_at]) // (entries.shape[axis_at] // blocks)).reshape((-1,) + (1,) * (entries.ndim - 1 - axis_at))

    near = jax.random.permutation(own_key, blocks)[block_of(target)]
    second = (block_of(target) + blocks // 2) % blocks
    return jnp.where((block_of(source) == near) | (block_of(source) == second), factor * entries, entries)


def levels(key, shape, cuts, least, largest):
    level = 1.0
    for position, blocks in cuts:
        steps = jax.random.uniform(jax.random.fold_in(jax.random.fold_in(key, 6), position), (blocks,), jnp.float32, least / len(cuts), largest / len(cuts))
        level = level * jnp.repeat(jnp.exp(steps), shape[position] // blocks).reshape((-1,) + (1,) * (len(shape) - 1 - position))
    return level


def centred(rng, dims, width, limit, cuts=(), held_as=jnp.bfloat16):
    result = width * jax.random.normal(rng, dims, jnp.float32)
    if cuts:
        result = result * levels(rng, dims, cuts, -0.22, 0.18)
    return jnp.clip(result, -limit, limit).astype(held_as)


def heavy_noise(stream_key, extent, scale, reach, cuts, heavy, kind=jnp.bfloat16):
    drawn = scale * jax.random.normal(stream_key, extent, jnp.float32)
    if cuts:
        drawn = drawn * levels(stream_key, extent, cuts, -0.22, 0.18)
    return jnp.clip(spiked(drawn, jax.random.fold_in(stream_key, 3), *heavy), -reach, reach).astype(kind)


def setup_inputs(seed: int = 0) -> dict:
    keys = jax.random.split(jax.random.key(seed), 12)
    return {
        "hidden": centred(keys[0], (SEQ_LEN, D), 1.0, 6.0, ((0, 16), (1, 8))),
        "norm_gain": jnp.clip(1.0 + 0.15 * jax.random.normal(keys[1], (HALF,), jnp.float32), 0.25, 1.75),
        "w_values": centred(keys[2], (HALF, INNER), HALF ** -0.5, 0.125, ((1, 8),)),
        "w_gates": centred(keys[3], (HALF, INNER), HALF ** -0.5, 0.125, ((1, 8),)),
        "w_control": centred(keys[4], (HALF, 2 * STATE + HEADS), (HALF * 8) ** -0.5, 0.046875),
        "dt_bias": jnp.clip(jax.random.uniform(keys[5], (HEADS,), jnp.float32, -1.0, 1.0), -1.0, 1.0),
        "decay_total": draw_decay_total(jax.random.fold_in(keys[11], 71), 0),
        "skip_gain": jnp.clip(jax.random.uniform(keys[7], (HEADS,), jnp.float32, 0.5, 2.0), 0.5, 2.0),
        "gate_gain": jnp.clip(1.0 + 0.15 * jax.random.normal(keys[8], (INNER,), jnp.float32), 0.25, 1.75),
        "w_out": heavy_noise(keys[9], (INNER, HALF), INNER ** -0.5, 0.125, ((0, 8),), (0, 1, 8, 2.0)),
        "doc_starts": draw_doc_starts(jax.random.fold_in(keys[11], 71), 0),
    }


norm_eps = 1e-05
highest = lax.Precision.HIGHEST

def segment_ids(positions, doc_starts):
    return (lax.optimization_barrier(jnp.sum((positions[:, None] >= doc_starts[None, :]).astype(jnp.int32), axis=1)) - 1).astype(jnp.int32)

def combine_stretches(earlier, latter):
    return (earlier[0] * latter[0], latter[0][..., None, :, None] * earlier[1] + latter[1])

def stretch_scan(inputs, log_decay, step_size, b_in, c_out, segment, seg_before):
    total_len, groups, head_width = inputs.shape
    blocks = total_len // STRETCH
    weighted = (inputs * step_size[:, :, None]).reshape(blocks, STRETCH, groups, head_width)
    running = jnp.cumsum(log_decay.reshape(blocks, STRETCH, groups), axis=1)
    stretch_total = running[:, -1]
    b_blocks = b_in.reshape(blocks, STRETCH, -1)
    c_blocks = c_out.reshape(blocks, STRETCH, -1)
    seg_blocks = segment.reshape(blocks, STRETCH)
    scores = jnp.einsum('kqn,ksn->kqs', c_blocks.astype(jnp.float32), b_blocks.astype(jnp.float32))
    by_group = jnp.transpose(running, (0, 2, 1))
    log_gaps = by_group[:, :, :, None] - by_group[:, :, None, :]
    index_rows = jnp.arange(STRETCH, dtype=jnp.int32)
    allowed = (index_rows[:, None] >= index_rows[None, :])[None] & (seg_blocks[:, :, None] == seg_blocks[:, None, :])
    decay_mask = jnp.exp(jnp.where(allowed[:, None], log_gaps, -jnp.inf))
    within = jnp.einsum('kgts,ksgw->ktgw', decay_mask * scores[:, None], weighted, precision=highest)
    toward_end = jnp.exp(stretch_total[:, None, :] - running) * (seg_blocks == seg_blocks[:, -1:]).astype(jnp.float32)[:, :, None]
    stretch_states = jnp.einsum('ksn,ksgw->kngw', b_blocks.astype(jnp.float32), weighted * toward_end[..., None], precision=highest)
    seg_prior = jnp.concatenate([jnp.reshape(seg_before, (1,)).astype(jnp.int32), seg_blocks[:-1, -1]])
    stretch_keep = jnp.exp(stretch_total) * (seg_blocks[:, -1] == seg_prior).astype(jnp.float32)[:, None]
    keep_incl, state_incl = lax.associative_scan(combine_stretches, (stretch_keep, stretch_states))
    state_prior = jnp.concatenate([jnp.zeros_like(stretch_states[:1]), state_incl[:-1]])
    reach_factor = jnp.exp(running) * (seg_blocks == seg_prior[:, None]).astype(jnp.float32)[:, :, None]
    carried = jnp.einsum('kqn,kngw->kqgw', c_blocks.astype(jnp.float32), state_prior, precision=highest) * reach_factor[..., None]
    return ((within + carried).reshape(total_len, groups, head_width), keep_incl[-1], state_incl[-1])

def strand_scan(values, control, segment, dt_bias, decay_total, skip_gain):
    length = values.shape[0]
    b_in = control[:, :STATE]
    c_out = control[:, STATE:2 * STATE]
    step_size = jax.nn.softplus(control[:, 2 * STATE:].astype(jnp.float32) + dt_bias)
    log_decay = -(decay_total / SEQ_LEN) * step_size
    group_size = math.gcd(HEADS, 8)
    group_count = HEADS // group_size
    inputs = values.astype(jnp.float32).reshape(length, group_count, group_size, HEAD_DIM).transpose(1, 0, 2, 3)
    decay_groups = log_decay.reshape(length, group_count, group_size).transpose(1, 0, 2)
    step_groups = step_size.reshape(length, group_count, group_size).transpose(1, 0, 2)
    skip_groups = skip_gain.reshape(group_count, group_size)
    no_segment = jnp.int32(-1)

    def scan_group(operands):
        part_in, part_decay, part_step, part_skip = operands
        forward = stretch_scan(part_in, part_decay, part_step, b_in, c_out, segment, no_segment)[0]
        backward = stretch_scan(part_in[::-1], part_decay[::-1], part_step[::-1], b_in[::-1], c_out[::-1], segment[::-1], no_segment)[0][::-1]
        direct = part_skip[None, :, None] * part_in
        return jnp.stack([forward + direct, backward + direct])
    scanned = lax.map(scan_group, (inputs, decay_groups, step_groups, skip_groups))
    return scanned.transpose(1, 2, 0, 3, 4).reshape(2, length, INNER).astype(jnp.bfloat16)

def reference(hidden, norm_gain, w_values, w_gates, w_control, dt_bias, decay_total, skip_gain, gate_gain, w_out, doc_starts):
    strands = jnp.stack([hidden[:, :HALF], hidden[:, HALF:][:, ::-1]])
    widened = strands.astype(jnp.float32)
    normed = (widened * lax.rsqrt(lax.optimization_barrier(jnp.mean(widened * widened, axis=-1, keepdims=True)) + norm_eps) * norm_gain).astype(jnp.bfloat16)
    normed_wide = normed.astype(jnp.float32)
    values = jnp.einsum('sth,he->ste', normed_wide, w_values.astype(jnp.float32)).astype(jnp.bfloat16)
    gates = jnp.einsum('sth,he->ste', normed_wide, w_gates.astype(jnp.float32)).astype(jnp.bfloat16)
    control = jnp.einsum('sth,he->ste', normed_wide, w_control.astype(jnp.float32)).astype(jnp.bfloat16)
    segment = segment_ids(jnp.arange(SEQ_LEN, dtype=jnp.int32), doc_starts)
    results = []
    for strand in range(2):
        scanned = strand_scan(values[strand], control[strand], segment, dt_bias, decay_total, skip_gain)
        gate_wide = gates[strand].astype(jnp.float32)
        activated = gate_wide * jax.nn.sigmoid(gate_wide)
        gated_values = scanned.astype(jnp.float32) * activated[None]
        scaled = gated_values * lax.rsqrt(lax.optimization_barrier(jnp.mean(gated_values * gated_values, axis=-1, keepdims=True)) + norm_eps) * gate_gain
        combined = (scaled[0] + scaled[1]).astype(jnp.bfloat16)
        results.append(jnp.dot(combined, w_out, preferred_element_type=jnp.float32))
    layer_out = jnp.concatenate([results[0], results[1][:, ::-1]], axis=1).astype(jnp.bfloat16)
    return layer_out
```

```python
import jax
import jax.numpy as jnp
from jax import lax
from jax.experimental import pallas as pl
from jax.experimental.pallas import tpu as pltpu
from jax.sharding import PartitionSpec as P

MESH = pl.DeviceIdType.MESH
F32 = jnp.float32
BF16 = jnp.bfloat16
HIGHEST = lax.Precision.HIGHEST

HEAD_DIM = 64
STATE = 128
CHUNK = 128
ROWS = 512
COLS = 512
HALF = 2048
HEADS = 64
NCHAN = 8
NSEQ = 16
CHUNKS = ROWS // CHUNK
PAIRS = COLS // 128
RB = 288
RA = ROWS - RB
RBH = RB // 2
RAH = RA // 2
GROUP = STATE // NSEQ
norm_eps = 1e-05


def dot(a, b):
    return jnp.dot(a, b, preferred_element_type=F32)


def dot_nt(a, b):
    return lax.dot_general(a, b, (((1,), (1,)), ((), ())), preferred_element_type=F32)


def dot_tn(a, b):
    return lax.dot_general(a, b, (((0,), (0,)), ((), ())), preferred_element_type=F32)


def iota(shape, dim):
    return lax.broadcasted_iota(jnp.int32, shape, dim)


def remote(src, dst, send_sem, recv_sem, device):
    return pltpu.make_async_remote_copy(
        src_ref=src,
        dst_ref=dst,
        send_sem=send_sem,
        recv_sem=recv_sem,
        device_id=device,
        device_id_type=MESH,
    )


def kernel(
    x_hbm, gain_ref, wv_hbm, wg_hbm, wc_hbm, bias_ref, decay_ref, skip_ref, ggain_ref, wo_hbm, docs,
    out_ref,
    x_v, wv, wg, wc, wo, gath, xg, acc_v, acc_g, acc_c, sumsq, rinv,
    c_sc, wval, val, l_sc, e_sc, reach, chunk_state, tot_sc, totx,
    st_send, st_recv, enter, en_send, en_recv, carry, y_f, y_b, params,
    ps_buf, ps_mine, comb, part, rb1, rb2, rb3, ra1, ra2, ra3,
    loc_sem, ag_send, ag_recv, s1_send, s1_recv, s2_send, s2_recv, ps_send, ps_recv, rs_send, rs_recv,
):
    seq = lax.axis_index("seq")
    chan = lax.axis_index("chan")
    yy = chan // 2
    zz = chan % 2

    def chan_of(dy, flip):
        return ((yy + dy) % 4) * 2 + (1 - zz if flip else zz)

    def slot_of(c):
        return jnp.where(c < 4, c, 11 - c)

    c_p, c_m, c_o = chan_of(1, False), chan_of(3, False), chan_of(0, True)
    c_q, c_pz, c_mz, c_qz = chan_of(2, False), chan_of(1, True), chan_of(3, True), chan_of(2, True)
    k_me, k_p, k_m, k_o = slot_of(chan), slot_of(c_p), slot_of(c_m), slot_of(c_o)
    k_q, k_pz, k_mz, k_qz = slot_of(c_q), slot_of(c_pz), slot_of(c_mz), slot_of(c_qz)
    to_p, to_m, to_o = {"chan": c_p}, {"chan": c_m}, {"chan": c_o}

    barrier = pltpu.get_barrier_semaphore()

    def greet_chan(k, carry_):
        pl.semaphore_signal(barrier, inc=1, device_id={"chan": (chan + k) % NCHAN}, device_id_type=MESH)
        return carry_

    def greet_seq(k, carry_):
        pl.semaphore_signal(barrier, inc=1, device_id={"seq": (seq + k) % NSEQ}, device_id_type=MESH)
        return carry_

    lax.fori_loop(1, NCHAN, greet_chan, 0)
    lax.fori_loop(1, NSEQ, greet_seq, 0)

    x_copy = pltpu.make_async_copy(x_hbm, x_v, loc_sem.at[0])
    x_copy.start()
    w_copies = [
        pltpu.make_async_copy(wv_hbm, wv, loc_sem.at[1]),
        pltpu.make_async_copy(wg_hbm, wg, loc_sem.at[2]),
        pltpu.make_async_copy(wc_hbm, wc, loc_sem.at[3]),
    ]
    for copy in w_copies:
        copy.start()
    wo_copies = [
        pltpu.make_async_copy(wo_hbm.at[:, k * COLS : (k + 1) * COLS], wo.at[k], loc_sem.at[4 + k])
        for k in range(4)
    ]
    for copy in wo_copies:
        copy.start()

    mirrored = chan >= 4
    col = iota((COLS, COLS), 1)
    wanted = jnp.where(mirrored, COLS - 1 - col, col)
    flip = jnp.where(iota((COLS, COLS), 0) == wanted, 1.0, 0.0).astype(BF16)
    x_copy.wait()
    gath[k_me] = dot(x_v[...], flip).astype(BF16)

    pl.semaphore_wait(barrier, NCHAN + NSEQ - 2)

    rows_b, rows_a = pl.ds(0, RB), pl.ds(RB, RA)
    rows_b1, rows_b2 = pl.ds(0, RBH), pl.ds(RBH, RBH)
    rows_a1, rows_a2 = pl.ds(RB, RAH), pl.ds(RB + RAH, RAH)
    started = []

    def ag(kind, slot, rows, device):
        part_ref = gath.at[slot, rows]
        copy = remote(part_ref, part_ref, ag_send.at[kind], ag_recv.at[kind], device)
        copy.start()
        started.append(copy)

    def ag_wait(kind, slot, rows):
        part_ref = gath.at[slot, rows]
        remote(part_ref, part_ref, ag_send.at[kind], ag_recv.at[kind], to_p).wait_recv()

    ag(11, k_me, rows_a, to_p)
    ag(12, k_me, rows_a, to_m)
    ag(0, k_me, rows_b, to_o)
    ag(1, k_me, rows_b, to_p)
    ag(2, k_me, rows_b, to_m)
    ag(10, k_me, rows_a, to_o)

    acc_v[...] = jnp.zeros_like(acc_v)
    acc_g[...] = jnp.zeros_like(acc_g)
    acc_c[...] = jnp.zeros_like(acc_c)
    sumsq[...] = jnp.zeros_like(sumsq)

    def project(slot):
        strand = slot // 4
        k = slot % 4
        gain = gain_ref[k]

        def scale_rows(i, carry_):
            rows = pl.ds(pl.multiple_of(i * 64, 64), 64)
            x = gath[slot, rows, :].astype(F32)
            xg[rows, :] = (x * gain).astype(BF16)
            sq = x * x
            sumsq[strand, rows, :] += sq[:, 0:128] + sq[:, 128:256] + sq[:, 256:384] + sq[:, 384:512]
            return carry_

        lax.fori_loop(0, ROWS // 64, scale_rows, 0)
        depth = pl.ds(pl.multiple_of(k * COLS, COLS), COLS)

        def multiply(i, carry_):
            rows = pl.ds(pl.multiple_of(i * 256, 256), 256)
            lhs = xg[rows, :]
            acc_v[strand, rows, :] += dot(lhs, wv[depth, :])
            acc_g[strand, rows, :] += dot(lhs, wg[depth, :])
            acc_c[strand, rows, :] += dot(lhs, wc[depth, :])
            return carry_

        lax.fori_loop(0, ROWS // 256, multiply, 0)

    for copy in w_copies:
        copy.wait()
    project(k_me)

    ag_wait(11, k_m, rows_a)
    ag(13, k_m, rows_a, to_o)
    ag(15, k_m, rows_a1, to_p)
    ag_wait(12, k_p, rows_a)
    ag(14, k_p, rows_a, to_o)
    ag(16, k_p, rows_a2, to_m)
    ag_wait(0, k_o, rows_b)
    ag(3, k_o, rows_b, to_p)
    ag(4, k_o, rows_b, to_m)
    ag_wait(1, k_m, rows_b)
    ag(5, k_m, rows_b1, to_p)
    ag_wait(2, k_p, rows_b)
    ag(6, k_p, rows_b2, to_m)
    ag_wait(15, k_q, rows_a1)
    ag(17, k_q, rows_a1, to_o)
    ag_wait(16, k_q, rows_a2)
    ag(9, k_q, rows_a2, to_o)
    ag_wait(10, k_o, rows_a)

    def project_first(i, carry_):
        project(jnp.where(i == 0, k_o, jnp.where(i == 1, k_m, k_p)))
        return carry_

    lax.fori_loop(0, 3, project_first, 0)
    ag_wait(3, k_mz, rows_b)
    ag(7, k_mz, rows_b1, to_p)
    ag_wait(4, k_pz, rows_b)
    ag(8, k_pz, rows_b2, to_m)
    ag_wait(13, k_mz, rows_a)
    ag_wait(14, k_pz, rows_a)
    ag_wait(5, k_q, rows_b1)
    ag_wait(6, k_q, rows_b2)

    def project_second(i, carry_):
        project(jnp.where(i == 0, k_mz, jnp.where(i == 1, k_pz, k_q)))
        return carry_

    lax.fori_loop(0, 3, project_second, 0)
    ag_wait(7, k_qz, rows_b1)
    ag_wait(8, k_qz, rows_b2)
    ag_wait(17, k_qz, rows_a1)
    ag_wait(9, k_qz, rows_a2)
    project(k_qz)

    for strand in range(2):
        for i in range(CHUNKS):
            rows = pl.ds(i * CHUNK, CHUNK)
            total = jnp.sum(sumsq[strand, rows, :], axis=1, keepdims=True)
            rinv[strand, rows, :] = jnp.broadcast_to(
                lax.rsqrt(total * (1.0 / HALF) + norm_eps), (CHUNK, 128)
            )

    first_head = chan * (COLS // HEAD_DIM)
    lane = iota((HEADS, 128), 1)
    pick = jnp.where((iota((HEADS, 128), 0) == first_head + lane) & (lane < COLS // HEAD_DIM), 1.0, 0.0)
    spread64 = jnp.where(
        iota((HEADS, COLS), 0) == first_head + iota((HEADS, COLS), 1) // HEAD_DIM, 1.0, 0.0
    )
    spread = jnp.where(iota((128, COLS), 0) == iota((128, COLS), 1) // HEAD_DIM, 1.0, 0.0)
    pick_b = pick.astype(BF16)
    spread_b = spread.astype(BF16)

    def exact(row, table):
        return jnp.dot(
            jnp.broadcast_to(row, (8, row.shape[1])), table, precision=HIGHEST, preferred_element_type=F32
        )

    params[0] = exact(bias_ref[...], pick)
    params[1] = exact(decay_ref[...], pick) * (-1.0 / (ROWS * NSEQ))
    skip_x = exact(skip_ref[...], spread64)[0:1]

    starts = [docs[k] for k in range(4)]
    base = seq * ROWS

    def seg_at(position):
        total = jnp.int32(0)
        for start in starts:
            total = total + jnp.where(position >= start, 1, 0)
        return total

    def same(a, b):
        return jnp.where(seg_at(a) == seg_at(b), 1.0, 0.0)

    def keep_f(begin, end):
        return same(end, begin - 1)

    def keep_b(begin, end):
        return same(begin, end + 1)

    sub = iota((CHUNK, CHUNK), 0)
    lan = iota((CHUNK, CHUNK), 1)
    lower = jnp.where(sub >= lan, 1.0, 0.0).astype(BF16)

    def states(i, carry_):
        s = i // CHUNKS
        c = i % CHUNKS
        rows = pl.ds(pl.multiple_of(c * CHUNK, CHUNK), CHUNK)
        begin = base + c * CHUNK
        end = begin + CHUNK - 1
        r = rinv[s, rows, :][:, 0:1]
        v = (acc_v[s, rows, :] * r).astype(BF16)
        val[s, rows, :] = v
        v32 = v.astype(F32)
        ctl = (acc_c[s, rows, :] * r).astype(BF16)
        b_in = ctl[:, 0:STATE]
        c_sc[s, rows, 0:STATE] = b_in
        c_sc[s, rows, STATE : 2 * STATE] = ctl[:, STATE : 2 * STATE]
        z = dot(ctl[:, 2 * STATE :], pick_b) + params[0, 0:1]
        step = jnp.maximum(z, 0.0) + jnp.log1p(jnp.exp(-jnp.abs(z)))
        log_rate = params[1, 0:1] * step
        p1 = log_rate.astype(BF16)
        rest = log_rate - p1.astype(F32)
        p2 = rest.astype(BF16)
        p3 = (rest - p2.astype(F32)).astype(BF16)
        run = dot(lower, p1) + dot(lower, p2) + dot(lower, p3)
        before = run - log_rate
        total = run[CHUNK - 1 : CHUNK, :]
        l_sc[s, rows, :] = run
        e_sc[s, rows, :] = before
        tot_sc[s, pl.ds(pl.multiple_of(c * 8, 8), 8), :] = jnp.broadcast_to(total, (8, 128))
        seg = seg_at(begin + sub)

        def mask(position):
            return jnp.where(seg == seg_at(position), 1.0, 0.0)

        out_f = jnp.exp(total - run) * mask(end)
        out_b = jnp.exp(before) * mask(begin)
        in_f = jnp.exp(run) * mask(begin - 1)
        in_b = jnp.exp(total - before) * mask(end + 1)
        wide = dot(
            jnp.concatenate([step, step * out_f, step * out_b, in_f, in_b], axis=0).astype(BF16), spread_b
        )
        wval[s, rows, :] = (wide[0:CHUNK] * v32).astype(BF16)
        weighted = jnp.concatenate(
            [wide[CHUNK : 2 * CHUNK] * v32, wide[2 * CHUNK : 3 * CHUNK] * v32], axis=1
        ).astype(BF16)
        reach[s, 0, rows, :] = wide[3 * CHUNK : 4 * CHUNK].astype(BF16)
        reach[s, 1, rows, :] = wide[4 * CHUNK : 5 * CHUNK].astype(BF16)
        chunk_state[i] = dot_tn(b_in, weighted)
        return carry_

    lax.fori_loop(0, 2 * CHUNKS, states, 0)

    pieces = []
    for s in range(2):
        totx[s] = jnp.dot(tot_sc[s], spread, precision=HIGHEST, preferred_element_type=F32)
        f = chunk_state[s * CHUNKS, :, 0:COLS]
        for c in range(1, CHUNKS):
            begin = base + c * CHUNK
            kept = jnp.exp(totx[s, c * 8 : c * 8 + 1, :]) * keep_f(begin, begin + CHUNK - 1)
            f = chunk_state[s * CHUNKS + c, :, 0:COLS] + kept * f
        b = chunk_state[s * CHUNKS + CHUNKS - 1, :, COLS:]
        for c in range(CHUNKS - 2, -1, -1):
            begin = base + c * CHUNK
            kept = jnp.exp(totx[s, c * 8 : c * 8 + 1, :]) * keep_b(begin, begin + CHUNK - 1)
            b = chunk_state[s * CHUNKS + c, :, COLS:] + kept * b
        st_send[:, s] = jnp.concatenate(
            [f.reshape(NSEQ, GROUP, COLS), b.reshape(NSEQ, GROUP, COLS)], axis=1
        ).astype(BF16)
        log_total = totx[s, 0:8, :] + totx[s, 8:16, :] + totx[s, 16:24, :] + totx[s, 24:32, :]
        t1 = log_total.astype(BF16).astype(F32)
        t2 = (log_total - t1).astype(BF16).astype(F32)
        t3 = log_total - t1 - t2
        row8 = iota((8, COLS), 0)
        pieces.append(jnp.where(row8 == 0, t1, jnp.where(row8 == 1, t2, jnp.where(row8 == 2, t3, 0.0))))
    logs = jnp.concatenate(pieces, axis=0).astype(BF16)

    def put_logs(j, carry_):
        st_send[j, 2] = logs
        return carry_

    lax.fori_loop(0, NSEQ, put_logs, 0)

    def send_state(k, carry_):
        peer = (seq + k) % NSEQ
        remote(
            st_send.at[peer], st_recv.at[seq], s1_send.at[k], s1_recv.at[k], {"seq": peer}
        ).start()
        return carry_

    lax.fori_loop(1, NSEQ, send_state, 0)
    own_state = pltpu.make_async_copy(st_send.at[seq], st_recv.at[seq], loc_sem.at[8])
    own_state.start()

    left = iota((CHUNK, 128), 1) < HEAD_DIM

    def within(i, carry_):
        s = i // CHUNKS
        c = i % CHUNKS
        rows = pl.ds(pl.multiple_of(c * CHUNK, CHUNK), CHUNK)
        begin = base + c * CHUNK
        scores = dot_nt(c_sc[s, rows, STATE : 2 * STATE], c_sc[s, rows, 0:STATE])
        scores = jnp.where(seg_at(begin + sub) == seg_at(begin + lan), scores, 0.0)
        run = l_sc[s, rows, :]
        before = e_sc[s, rows, :]
        run_t = run.T
        before_t = before.T
        zero = jnp.zeros((CHUNK, CHUNK), F32)
        for pair in range(PAIRS):
            fs, bs = [], []
            for h in (2 * pair, 2 * pair + 1):
                gap = jnp.where(
                    sub >= lan,
                    run[:, h : h + 1] - run_t[h : h + 1, :],
                    before_t[h : h + 1, :] - before[:, h : h + 1],
                )
                g = jnp.exp(gap) * scores
                fs.append(jnp.where(sub >= lan, g, zero))
                bs.append(jnp.where(sub <= lan, g, zero))
            lhs = jnp.concatenate(
                [jnp.concatenate(fs, axis=1), jnp.concatenate(bs, axis=1)], axis=0
            ).astype(BF16)
            lanes = slice(pair * 128, pair * 128 + 128)
            w = wval[s, rows, lanes].astype(F32)
            rhs = jnp.concatenate([jnp.where(left, w, 0.0), jnp.where(left, 0.0, w)], axis=0).astype(BF16)
            y = dot(lhs, rhs)
            direct = skip_x[:, lanes] * val[s, rows, lanes].astype(F32)
            y_f[s, rows, lanes] = y[0:CHUNK] + direct
            y_b[s, rows, lanes] = y[CHUNK:] + direct
        return carry_

    lax.fori_loop(0, CHUNKS, within, 0)

    own_state.wait()

    def await_state(k, carry_):
        src = (seq + NSEQ - k) % NSEQ
        remote(
            st_send.at[src], st_recv.at[src], s1_send.at[k], s1_recv.at[k], {"seq": src}
        ).wait_recv()
        return carry_

    lax.fori_loop(1, NSEQ, await_state, 0)
    carry[...] = jnp.zeros_like(carry)

    def scan_f(d, carry_):
        begin = d * ROWS
        kept = keep_f(begin, begin + ROWS - 1)
        lg = st_recv[d, 2].astype(F32)
        for s in range(2):
            lt = lg[8 * s : 8 * s + 1] + lg[8 * s + 1 : 8 * s + 2] + lg[8 * s + 2 : 8 * s + 3]
            now = carry[s]
            enter[d, s, 0] = now
            carry[s] = st_recv[d, s].astype(F32)[0:GROUP] + jnp.exp(lt) * kept * now
        return carry_

    def scan_b(j, carry_):
        d = NSEQ - 1 - j
        begin = d * ROWS
        kept = keep_b(begin, begin + ROWS - 1)
        lg = st_recv[d, 2].astype(F32)
        for s in range(2):
            lt = lg[8 * s : 8 * s + 1] + lg[8 * s + 1 : 8 * s + 2] + lg[8 * s + 2 : 8 * s + 3]
            now = carry[2 + s]
            enter[d, s, 1] = now
            carry[2 + s] = st_recv[d, s].astype(F32)[GROUP : 2 * GROUP] + jnp.exp(lt) * kept * now
        return carry_

    lax.fori_loop(0, NSEQ, scan_f, 0)
    lax.fori_loop(0, NSEQ, scan_b, 0)

    def pack(d, carry_):
        for s in range(2):
            en_send[d, s] = jnp.concatenate([enter[d, s, 0], enter[d, s, 1]], axis=0).astype(BF16)
        return carry_

    lax.fori_loop(0, NSEQ, pack, 0)

    def send_enter(k, carry_):
        peer = (seq + k) % NSEQ
        remote(
            en_send.at[peer], en_recv.at[seq], s2_send.at[k], s2_recv.at[k], {"seq": peer}
        ).start()
        return carry_

    lax.fori_loop(1, NSEQ, send_enter, 0)
    own_enter = pltpu.make_async_copy(en_send.at[seq], en_recv.at[seq], loc_sem.at[9])
    own_enter.start()

    lax.fori_loop(CHUNKS, 2 * CHUNKS, within, 0)

    def activate(i, carry_):
        s = i // CHUNKS
        rows = pl.ds(pl.multiple_of((i % CHUNKS) * CHUNK, CHUNK), CHUNK)
        g = (acc_g[s, rows, :] * rinv[s, rows, :][:, 0:1]).astype(BF16).astype(F32)
        acc_g[s, rows, :] = g / (1.0 + jnp.exp(-g))
        return carry_

    lax.fori_loop(0, 2 * CHUNKS, activate, 0)

    own_enter.wait()

    def await_enter(k, carry_):
        src = (seq + NSEQ - k) % NSEQ
        remote(
            en_send.at[src], en_recv.at[src], s2_send.at[k], s2_recv.at[k], {"seq": src}
        ).wait_recv()
        return carry_

    lax.fori_loop(1, NSEQ, await_enter, 0)

    for s in range(2):
        both = en_recv[:, s].astype(F32)
        f = both[:, 0:GROUP].reshape(STATE, COLS)
        b = both[:, GROUP : 2 * GROUP].reshape(STATE, COLS)
        for c in range(CHUNKS):
            rows = pl.ds(c * CHUNK, CHUNK)
            begin = base + c * CHUNK
            cc = c_sc[s, rows, STATE : 2 * STATE]
            y_f[s, rows, :] += dot(cc, f.astype(BF16)) * reach[s, 0, rows, :].astype(F32)
            if c < CHUNKS - 1:
                kept = jnp.exp(totx[s, c * 8 : c * 8 + 1, :]) * keep_f(begin, begin + CHUNK - 1)
                f = chunk_state[s * CHUNKS + c, :, 0:COLS] + kept * f
        for c in range(CHUNKS - 1, -1, -1):
            rows = pl.ds(c * CHUNK, CHUNK)
            begin = base + c * CHUNK
            cc = c_sc[s, rows, STATE : 2 * STATE]
            y_b[s, rows, :] += dot(cc, b.astype(BF16)) * reach[s, 1, rows, :].astype(F32)
            if c > 0:
                kept = jnp.exp(totx[s, c * 8 : c * 8 + 1, :]) * keep_b(begin, begin + CHUNK - 1)
                b = chunk_state[s * CHUNKS + c, :, COLS:] + kept * b

    ones = jnp.ones((8, COLS), BF16)
    row8 = iota((8, CHUNK), 0)

    def gate(c, carry_):
        rows = pl.ds(pl.multiple_of(c * CHUNK, CHUNK), CHUNK)
        sums = jnp.zeros((8, CHUNK), F32)
        for s in range(2):
            act = acc_g[s, rows, :]
            for d, y in enumerate((y_f, y_b)):
                v = y[s, rows, :] * act
                y[s, rows, :] = v
                sq = v * v
                hi = sq.astype(BF16)
                lo = (sq - hi.astype(F32)).astype(BF16)
                sums = sums + jnp.where(row8 == 2 * s + d, dot_nt(ones, hi) + dot_nt(ones, lo), 0.0)
        ps_mine[:, pl.ds(pl.multiple_of(c * CHUNK, CHUNK), CHUNK)] = sums
        return carry_

    lax.fori_loop(0, CHUNKS, gate, 0)

    def send_sums(k, carry_):
        remote(
            ps_mine, ps_buf.at[k], ps_send.at[k], ps_recv.at[k], {"chan": (chan + k) % NCHAN}
        ).start()
        return carry_

    def await_sums(k, carry_):
        remote(
            ps_mine, ps_buf.at[k], ps_send.at[k], ps_recv.at[k], {"chan": (chan + k) % NCHAN}
        ).wait_recv()
        return carry_

    lax.fori_loop(1, NCHAN, send_sums, 0)
    lax.fori_loop(1, NCHAN, await_sums, 0)
    sums = ps_mine[...]
    for k in range(1, NCHAN):
        sums = sums + ps_buf[k]
    scale = lax.rsqrt(sums * (1.0 / (COLS * NCHAN)) + norm_eps)
    scale = jnp.concatenate([scale, jnp.zeros((CHUNK - 8, ROWS), F32)], axis=0)
    for c in range(CHUNKS):
        rinv[0, c * CHUNK : (c + 1) * CHUNK, :] = scale[:, c * CHUNK : (c + 1) * CHUNK].T

    def combine(c, carry_):
        rows = pl.ds(pl.multiple_of(c * CHUNK, CHUNK), CHUNK)
        r = rinv[0, rows, :]
        for s in range(2):
            both = y_f[s, rows, :] * r[:, 2 * s : 2 * s + 1] + y_b[s, rows, :] * r[:, 2 * s + 1 : 2 * s + 2]
            comb[s, rows, :] = (both * ggain_ref[...]).astype(BF16)
        return carry_

    lax.fori_loop(0, CHUNKS, combine, 0)

    for copy in wo_copies:
        copy.wait()

    def out_block(slot):
        def block(i, carry_):
            rows = pl.ds(pl.multiple_of(i * 256, 256), 256)
            part[slot, rows, :] = dot(comb[slot // 4, rows, :], wo[slot % 4]).astype(BF16)
            return carry_

        lax.fori_loop(0, ROWS // 256, block, 0)

    def rs(kind, slot, rows, dst, device):
        copy = remote(part.at[slot, rows], dst, rs_send.at[kind], rs_recv.at[kind], device)
        copy.start()
        started.append(copy)

    def rs_wait(kind, slot, rows, dst):
        remote(part.at[slot, rows], dst, rs_send.at[kind], rs_recv.at[kind], to_p).wait_recv()

    def add(slot, rows, *arrived):
        total = part[slot, rows, :].astype(F32)
        for ref in arrived:
            total = total + ref[...].astype(F32)
        part[slot, rows, :] = total.astype(BF16)

    def out_first(i, carry_):
        out_block(jnp.where(i == 0, k_qz, k_q))
        return carry_

    def out_second(i, carry_):
        out_block(jnp.where(i == 0, k_mz, jnp.where(i == 1, k_pz, k_o)))
        return carry_

    def out_third(i, carry_):
        out_block(jnp.where(i == 0, k_m, jnp.where(i == 1, k_p, k_me)))
        return carry_

    lax.fori_loop(0, 2, out_first, 0)
    rs(12, k_qz, rows_a, ra1.at[3], to_o)
    rs(1, k_qz, rows_b1, rb1.at[0, 1], to_m)
    rs(3, k_qz, rows_b2, rb1.at[1, 1], to_p)
    rs(0, k_q, rows_b1, rb1.at[0, 0], to_m)
    rs(2, k_q, rows_b2, rb1.at[1, 0], to_p)
    lax.fori_loop(0, 3, out_second, 0)
    rs(10, k_mz, rows_a, ra1.at[1], to_o)
    rs(11, k_pz, rows_a, ra1.at[2], to_o)
    rs(9, k_o, rows_a, ra1.at[0], to_o)
    rs_wait(1, k_mz, rows_b1, rb1.at[0, 1])
    add(k_mz, rows_b1, rb1.at[0, 1])
    rs(5, k_mz, rows_b, rb2.at[0, 1], to_m)
    rs_wait(3, k_pz, rows_b2, rb1.at[1, 1])
    add(k_pz, rows_b2, rb1.at[1, 1])
    rs(7, k_pz, rows_b, rb2.at[1, 1], to_p)
    lax.fori_loop(0, 3, out_third, 0)
    rs_wait(0, k_m, rows_b1, rb1.at[0, 0])
    add(k_m, rows_b1, rb1.at[0, 0])
    rs(4, k_m, rows_b, rb2.at[0, 0], to_m)
    rs_wait(2, k_p, rows_b2, rb1.at[1, 0])
    add(k_p, rows_b2, rb1.at[1, 0])
    rs(6, k_p, rows_b, rb2.at[1, 0], to_p)
    rs_wait(12, k_q, rows_a, ra1.at[3])
    add(k_q, rows_a, ra1.at[3])
    rs(13, k_q, rows_a1, ra2.at[0], to_m)
    rs(14, k_q, rows_a2, ra2.at[1], to_p)
    rs_wait(5, k_o, rows_b, rb2.at[0, 1])
    rs_wait(7, k_o, rows_b, rb2.at[1, 1])
    add(k_o, rows_b, rb2.at[0, 1], rb2.at[1, 1])
    rs(8, k_o, rows_b, rb3, to_o)
    rs_wait(10, k_m, rows_a, ra1.at[1])
    add(k_m, rows_a, ra1.at[1])
    rs_wait(13, k_m, rows_a1, ra2.at[0])
    add(k_m, rows_a1, ra2.at[0])
    rs(15, k_m, rows_a, ra3.at[0], to_m)
    rs_wait(11, k_p, rows_a, ra1.at[2])
    add(k_p, rows_a, ra1.at[2])
    rs_wait(14, k_p, rows_a2, ra2.at[1])
    add(k_p, rows_a2, ra2.at[1])
    rs(16, k_p, rows_a, ra3.at[1], to_p)
    rs_wait(9, k_me, rows_a, ra1.at[0])
    rs_wait(4, k_me, rows_b, rb2.at[0, 0])
    rs_wait(6, k_me, rows_b, rb2.at[1, 0])
    rs_wait(8, k_me, rows_b, rb3)
    add(k_me, rows_b, rb2.at[0, 0], rb2.at[1, 0], rb3)
    rs_wait(15, k_me, rows_a, ra3.at[0])
    rs_wait(16, k_me, rows_a, ra3.at[1])
    add(k_me, rows_a, ra1.at[0], ra3.at[0], ra3.at[1])
    out_ref[...] = dot(part[k_me], flip).astype(BF16)

    for copy in started:
        copy.wait_send()

    def sent_seq(k, carry_):
        peer = (seq + k) % NSEQ
        remote(st_send.at[peer], st_recv.at[seq], s1_send.at[k], s1_recv.at[k], {"seq": peer}).wait_send()
        remote(en_send.at[peer], en_recv.at[seq], s2_send.at[k], s2_recv.at[k], {"seq": peer}).wait_send()
        return carry_

    def sent_chan(k, carry_):
        remote(
            ps_mine, ps_buf.at[k], ps_send.at[k], ps_recv.at[k], {"chan": (chan + k) % NCHAN}
        ).wait_send()
        return carry_

    lax.fori_loop(1, NSEQ, sent_seq, 0)
    lax.fori_loop(1, NCHAN, sent_chan, 0)


def local(
    hidden, norm_gain, w_values, w_gates, w_control, dt_bias, decay_total, skip_gain, gate_gain, w_out, doc_starts
):
    vmem = pl.BlockSpec(memory_space=pltpu.VMEM)
    hbm = pl.BlockSpec(memory_space=pl.ANY)
    smem = pl.BlockSpec(memory_space=pltpu.SMEM)
    dma = pltpu.SemaphoreType.DMA
    scratch = [
        pltpu.VMEM((ROWS, COLS), BF16),
        pltpu.VMEM((HALF, COLS), BF16),
        pltpu.VMEM((HALF, COLS), BF16),
        pltpu.VMEM((HALF, 2 * STATE + HEADS), BF16),
        pltpu.VMEM((4, COLS, COLS), BF16),
        pltpu.VMEM((NCHAN, ROWS, COLS), BF16),
        pltpu.VMEM((ROWS, COLS), BF16),
        pltpu.VMEM((2, ROWS, COLS), F32),
        pltpu.VMEM((2, ROWS, COLS), F32),
        pltpu.VMEM((2, ROWS, 2 * STATE + HEADS), F32),
        pltpu.VMEM((2, ROWS, 128), F32),
        pltpu.VMEM((2, ROWS, 128), F32),
        pltpu.VMEM((2, ROWS, 2 * STATE), BF16),
        pltpu.VMEM((2, ROWS, COLS), BF16),
        pltpu.VMEM((2, ROWS, COLS), BF16),
        pltpu.VMEM((2, ROWS, 128), F32),
        pltpu.VMEM((2, ROWS, 128), F32),
        pltpu.VMEM((2, 2, ROWS, COLS), BF16),
        pltpu.VMEM((2 * CHUNKS, STATE, 2 * COLS), F32),
        pltpu.VMEM((2, 8 * CHUNKS, 128), F32),
        pltpu.VMEM((2, 8 * CHUNKS, COLS), F32),
        pltpu.VMEM((NSEQ, 3, 2 * GROUP, COLS), BF16),
        pltpu.VMEM((NSEQ, 3, 2 * GROUP, COLS), BF16),
        pltpu.VMEM((NSEQ, 2, 2, GROUP, COLS), F32),
        pltpu.VMEM((NSEQ, 2, 2 * GROUP, COLS), BF16),
        pltpu.VMEM((NSEQ, 2, 2 * GROUP, COLS), BF16),
        pltpu.VMEM((4, GROUP, COLS), F32),
        pltpu.VMEM((2, ROWS, COLS), F32),
        pltpu.VMEM((2, ROWS, COLS), F32),
        pltpu.VMEM((2, 8, 128), F32),
        pltpu.VMEM((NCHAN, 8, ROWS), F32),
        pltpu.VMEM((8, ROWS), F32),
        pltpu.VMEM((2, ROWS, COLS), BF16),
        pltpu.VMEM((NCHAN, ROWS, COLS), BF16),
        pltpu.VMEM((2, 2, RBH, COLS), BF16),
        pltpu.VMEM((2, 2, RB, COLS), BF16),
        pltpu.VMEM((RB, COLS), BF16),
        pltpu.VMEM((4, RA, COLS), BF16),
        pltpu.VMEM((2, RAH, COLS), BF16),
        pltpu.VMEM((2, RA, COLS), BF16),
        dma((10,)),
        dma((18,)),
        dma((18,)),
        dma((NSEQ,)),
        dma((NSEQ,)),
        dma((NSEQ,)),
        dma((NSEQ,)),
        dma((NCHAN,)),
        dma((NCHAN,)),
        dma((17,)),
        dma((17,)),
    ]
    return pl.pallas_call(
        kernel,
        name="mixer",
        out_shape=jax.ShapeDtypeStruct((ROWS, COLS), BF16),
        in_specs=[hbm, vmem, hbm, hbm, hbm, vmem, vmem, vmem, vmem, hbm, smem],
        out_specs=vmem,
        scratch_shapes=scratch,
        compiler_params=pltpu.CompilerParams(
            collective_id=0, has_side_effects=True, vmem_limit_bytes=60 * 2**20
        ),
    )(
        hidden,
        norm_gain.reshape(4, 1, COLS),
        w_values,
        w_gates,
        w_control,
        dt_bias.reshape(1, HEADS),
        decay_total.reshape(1, HEADS),
        skip_gain.reshape(1, HEADS),
        gate_gain.reshape(1, COLS),
        w_out,
        doc_starts,
    )


def solution(mesh):
    in_specs = (
        P("seq", "chan"),
        P(),
        P(None, "chan"),
        P(None, "chan"),
        P(),
        P(),
        P(),
        P(),
        P("chan"),
        P("chan", None),
        P(),
    )
    return jax.shard_map(local, mesh=mesh, in_specs=in_specs, out_specs=P("seq", "chan"), check_vma=False)
```

```python
import jax
import jax.numpy as jnp
from jax import lax
from jax.experimental import pallas as pl
from jax.experimental.pallas import tpu as pltpu
from jax.sharding import PartitionSpec as P

MESH = pl.DeviceIdType.MESH
F32 = jnp.float32
BF16 = jnp.bfloat16
HIGHEST = lax.Precision.HIGHEST

HEAD_DIM = 64
STATE = 128
CHUNK = 128
ROWS = 512
COLS = 512
HALF = 2048
HEADS = 64
NCHAN = 8
NSEQ = 16
CHUNKS = ROWS // CHUNK
PAIRS = COLS // 128
BLOCK_HEADS = COLS // HEAD_DIM
GROUP = STATE // NSEQ
HALF_ROWS = ROWS // 2
CTRL = 2 * STATE + HEADS
LOG2E = 1.4426950408889634
norm_eps = 1e-05


def dot(a, b):
    return jnp.dot(a, b, preferred_element_type=F32)


def dot_nt(a, b):
    return lax.dot_general(a, b, (((1,), (1,)), ((), ())), preferred_element_type=F32)


def dot_tn(a, b):
    return lax.dot_general(a, b, (((0,), (0,)), ((), ())), preferred_element_type=F32)


def exact(rows, table):
    return jnp.dot(rows, table, precision=HIGHEST, preferred_element_type=F32)


def iota(shape, dim):
    return lax.broadcasted_iota(jnp.int32, shape, dim)


def remote(src, dst, send_sem, recv_sem, device):
    return pltpu.make_async_remote_copy(
        src_ref=src,
        dst_ref=dst,
        send_sem=send_sem,
        recv_sem=recv_sem,
        device_id=device,
        device_id_type=MESH,
    )


def kernel(
    x_hbm, gain_ref, wv_hbm, wg_hbm, wc_hbm, bias_ref, decay_ref, skip_ref, ggain_ref, wo_hbm, docs,
    out_ref,
    x_v, wv, wg, wc, wo, gg, gath, xg, sumsq, rinv,
    c_sc, factors, scores_sc, l_sc, e_sc, lt_sc, et_sc, wval, val, act, reach, chunk_state, tot_sc, totx,
    log_recv, keep_x, st_send, st_recv, enter, en_send, en_recv, y_f, y_b,
    ps_buf, ps_mine, comb, part, rs_buf, relay,
    loc_sem, ag_send, ag_recv, w_send, w_recv, s0_send, s0_recv, s1_send, s1_recv, s2_send, s2_recv,
    ps_send, ps_recv, rs_send, rs_recv,
):
    seq = lax.axis_index("seq")
    chan = lax.axis_index("chan")
    yy = chan // 2
    zz = chan % 2
    y_near = yy + 1 - 2 * (yy % 2)
    c_n = y_near * 2 + zz
    c_o = yy * 2 + 1 - zz
    c_d = y_near * 2 + 1 - zz
    c_w = (3 - yy) * 2 + zz
    mirrored = chan >= 4

    def block_of(c):
        return jnp.where(mirrored, 7 - c, c)

    k_me, k_n, k_o, k_d = block_of(chan), block_of(c_n), block_of(c_o), block_of(c_d)
    to_n, to_o, to_d, to_w = {"chan": c_n}, {"chan": c_o}, {"chan": c_d}, {"chan": c_w}
    to_right, to_left = {"seq": (seq + 4) % NSEQ}, {"seq": (seq + 12) % NSEQ}
    to_twin = {"seq": seq + 1 - 2 * (seq % 2)}
    q_me = (seq // 4) * 2 + seq % 2
    q_twin = (seq // 4) * 2 + 1 - seq % 2

    barrier = pltpu.get_barrier_semaphore()
    for device in (to_n, to_o, to_d, to_w):
        pl.semaphore_signal(barrier, inc=1, device_id=device, device_id_type=MESH)

    def greet_seq(k, carry_):
        pl.semaphore_signal(barrier, inc=1, device_id={"seq": (seq + k) % NSEQ}, device_id_type=MESH)
        return carry_

    lax.fori_loop(1, NSEQ, greet_seq, 0)

    x_copy = pltpu.make_async_copy(x_hbm, x_v, loc_sem.at[0])
    x_copy.start()
    v_copy = pltpu.make_async_copy(wv_hbm, wv.at[0], loc_sem.at[1])
    c_copy = pltpu.make_async_copy(wc_hbm, wc, loc_sem.at[2])
    g_copy = pltpu.make_async_copy(wg_hbm, wg.at[0], loc_sem.at[3])
    o_copy = pltpu.make_async_copy(wo_hbm, wo.at[0], loc_sem.at[4])

    col = iota((COLS, COLS), 1)
    wanted = jnp.where(mirrored, COLS - 1 - col, col)
    flip = jnp.where(iota((COLS, COLS), 0) == wanted, 1.0, 0.0).astype(BF16)
    x_copy.wait()
    gath[k_me] = dot(x_v[...], flip).astype(BF16)
    gg[0] = ggain_ref[...]

    pl.semaphore_wait(barrier, 4 + NSEQ - 1)

    h1, h2 = pl.ds(0, HALF_ROWS), pl.ds(HALF_ROWS, HALF_ROWS)
    whole = pl.ds(0, ROWS)
    started = []

    def send(src, dst, send_sem, recv_sem, device):
        copy = remote(src, dst, send_sem, recv_sem, device)
        copy.start()
        started.append(copy)

    def ag(kind, block, rows, device):
        ref = gath.at[block, rows]
        send(ref, ref, ag_send.at[kind], ag_recv.at[kind], device)

    def ag_wait(kind, block, rows):
        ref = gath.at[block, rows]
        remote(ref, ref, ag_send.at[kind], ag_recv.at[kind], to_n).wait_recv()

    tensors = ((wv_hbm, wv, HALF // 8), (wg_hbm, wg, HALF // 8), (wo_hbm, wo, COLS // 8))

    def w_rows(t, dx, twin, half):
        size = tensors[t][2]
        q = ((q_twin if twin else q_me) + 2 * dx) % 8
        if half is None:
            return pl.ds(pl.multiple_of(q * size, size), size)
        return pl.ds(pl.multiple_of(q * size + half * (size // 2), size // 2), size // 2)

    def w_from_partner(t):
        hbm, buf, _ = tensors[t]
        rows = w_rows(t, 0, False, None)
        send(hbm.at[rows], buf.at[1, rows], w_send.at[t, 0], w_recv.at[t, 0], to_w)

    def w_on(t, kind, dx, half, device):
        ref = tensors[t][1].at[1, w_rows(t, dx, False, half)]
        send(ref, ref, w_send.at[t, kind], w_recv.at[t, kind], device)

    def w_wait(t, kind, dx, twin, half):
        ref = tensors[t][1].at[1, w_rows(t, dx, twin, half)]
        remote(ref, ref, w_send.at[t, kind], w_recv.at[t, kind], to_w).wait_recv()

    def w_stage1(t):
        w_wait(t, 0, 0, False, None)
        w_on(t, 1, 0, None, to_right)
        w_on(t, 2, 0, None, to_left)
        w_on(t, 3, 0, None, to_twin)

    def w_stage2(t):
        w_wait(t, 1, 3, False, None)
        w_on(t, 4, 3, 0, to_right)
        w_on(t, 5, 3, None, to_twin)
        w_wait(t, 2, 1, False, None)
        w_on(t, 6, 1, 1, to_left)
        w_on(t, 7, 1, None, to_twin)

    def w_stage3(t):
        w_wait(t, 4, 2, False, 0)
        w_on(t, 8, 2, 0, to_twin)
        w_wait(t, 6, 2, False, 1)
        w_on(t, 9, 2, 1, to_twin)

    def w_finish(t):
        w_wait(t, 3, 0, True, None)
        w_wait(t, 5, 3, True, None)
        w_wait(t, 7, 1, True, None)
        w_wait(t, 8, 2, True, 0)
        w_wait(t, 9, 2, True, 1)

    ag(0, k_me, h1, to_n)
    ag(2, k_me, h2, to_o)
    w_from_partner(0)
    ag(1, k_me, h2, to_n)
    ag(3, k_me, h1, to_o)
    w_from_partner(1)
    send(ggain_ref, gg.at[1], ag_send.at[6], ag_recv.at[6], to_w)
    for copy in (v_copy, c_copy, g_copy, o_copy):
        copy.start()

    def scale_block(k):
        gain = gain_ref[k]
        lanes = pl.ds(pl.multiple_of(k * COLS, COLS), COLS)

        def scale_rows(i, carry_):
            rows = pl.ds(pl.multiple_of(i * 64, 64), 64)
            x = gath[k, rows, :].astype(F32)
            xg[rows, lanes] = (x * gain).astype(BF16)
            sq = x * x
            sumsq[rows, :] += sq[:, 0:128] + sq[:, 128:256] + sq[:, 256:384] + sq[:, 384:512]
            return carry_

        lax.fori_loop(0, ROWS // 64, scale_rows, 0)

    sumsq[...] = jnp.zeros_like(sumsq)
    scale_block(k_me)

    lane = iota((HEADS, 128), 1)
    head = iota((HEADS, 128), 0)
    picked = ((head == chan * BLOCK_HEADS + lane) & (lane < BLOCK_HEADS)) | (
        (head == (c_w - 1) * BLOCK_HEADS + lane) & (lane >= BLOCK_HEADS) & (lane < 2 * BLOCK_HEADS)
    )
    pick = jnp.where(picked, 1.0, 0.0)
    spread = jnp.where(iota((128, 2 * COLS), 0) == iota((128, 2 * COLS), 1) // HEAD_DIM, 1.0, 0.0)
    pick_b = pick.astype(BF16)
    spread_b = spread.astype(BF16)

    def head_row(ref):
        return exact(jnp.broadcast_to(ref[...], (8, HEADS)), pick)

    bias = head_row(bias_ref)[0:1]
    slope = head_row(decay_ref)[0:1] * (-LOG2E / (ROWS * NSEQ))
    skip_x = exact(head_row(skip_ref), spread)[0:1]

    starts = [docs[k] for k in range(4)]
    base = seq * ROWS

    def seg_at(position):
        total = jnp.int32(0)
        for start in starts:
            total = total + jnp.where(position >= start, 1, 0)
        return total

    def same(a, b):
        return jnp.where(seg_at(a) == seg_at(b), 1.0, 0.0)

    def keep_f(begin, end):
        return same(end, begin - 1)

    def keep_b(begin, end):
        return same(begin, end + 1)

    sub = iota((CHUNK, CHUNK), 0)
    lan = iota((CHUNK, CHUNK), 1)
    lower = jnp.where(sub >= lan, 1.0, 0.0).astype(BF16)
    upper = jnp.where(sub <= lan, 1.0, 0.0).astype(BF16)

    ag_wait(0, k_n, h1)
    ag(4, k_n, h1, to_o)
    ag_wait(2, k_o, h2)
    ag(5, k_o, h2, to_n)
    w_stage1(0)
    ag_wait(1, k_n, h2)
    scale_block(k_n)
    ag_wait(3, k_o, h1)
    scale_block(k_o)
    w_stage1(1)
    w_from_partner(2)
    w_stage2(0)
    w_stage3(0)
    ag_wait(4, k_d, h1)
    ag_wait(5, k_d, h2)
    scale_block(k_d)

    for i in range(CHUNKS):
        rows = pl.ds(i * CHUNK, CHUNK)
        total = jnp.sum(sumsq[rows, :], axis=1, keepdims=True)
        rinv[rows, :] = jnp.broadcast_to(lax.rsqrt(total * (1.0 / HALF) + norm_eps), (CHUNK, 128))

    def project_control(i, carry_):
        rows = pl.ds(pl.multiple_of(i * 256, 256), 256)
        c_sc[rows, :] = (dot_nt(xg[rows, :], wc[...]) * rinv[rows, :][:, 0:1]).astype(BF16)
        return carry_

    def project_values(blk):
        def go(i, carry_):
            rows = pl.ds(pl.multiple_of(i * 256, 256), 256)
            val[blk, rows, :] = (dot(xg[rows, :], wv[blk]) * rinv[rows, :][:, 0:1]).astype(BF16)
            return carry_

        lax.fori_loop(0, 2, go, 0)

    def project_gates(blk):
        def go(i, carry_):
            rows = pl.ds(pl.multiple_of(i * 256, 256), 256)
            g = (dot(xg[rows, :], wg[blk]) * rinv[rows, :][:, 0:1]).astype(BF16).astype(F32)
            act[blk, rows, :] = g / (1.0 + jnp.exp(-g))
            return carry_

        lax.fori_loop(0, 2, go, 0)

    c_copy.wait()
    lax.fori_loop(0, 2, project_control, 0)
    v_copy.wait()
    project_values(0)
    w_stage2(1)
    w_stage1(2)

    def compact(c, carry_):
        rows = pl.ds(pl.multiple_of(c * CHUNK, CHUNK), CHUNK)
        begin = base + c * CHUNK
        end = begin + CHUNK - 1
        ctl = c_sc[rows, :]
        z = dot(ctl[:, 2 * STATE :], pick_b) + bias
        step = jnp.maximum(z, 0.0) + jnp.log1p(jnp.exp(-jnp.abs(z)))
        log_rate = slope * step
        p1 = log_rate.astype(BF16)
        rest = log_rate - p1.astype(F32)
        p2 = rest.astype(BF16)
        p3 = (rest - p2.astype(F32)).astype(BF16)
        run = dot(lower, p1) + dot(lower, p2) + dot(lower, p3)
        before = run - log_rate
        total = run[CHUNK - 1 : CHUNK, :]
        l_sc[0, rows, :] = run
        e_sc[0, rows, :] = before
        l_sc[1, rows, :] = pltpu.roll(run, 128 - BLOCK_HEADS, 1)
        e_sc[1, rows, :] = pltpu.roll(before, 128 - BLOCK_HEADS, 1)
        run_t = run.T
        before_t = before.T
        for blk in range(2):
            lt_sc[blk, c] = run_t[blk * BLOCK_HEADS : (blk + 1) * BLOCK_HEADS, :]
            et_sc[blk, c] = before_t[blk * BLOCK_HEADS : (blk + 1) * BLOCK_HEADS, :]
        tot_sc[c] = jnp.broadcast_to(total, (8, 128))
        seg = seg_at(begin + sub)

        def mask(position):
            return jnp.where(seg == seg_at(position), 1.0, 0.0)

        out_f = jnp.exp2(total - run) * mask(end)
        out_b = jnp.exp2(before) * mask(begin)
        in_f = jnp.exp2(run) * mask(begin - 1)
        in_b = jnp.exp2(total - before) * mask(end + 1)
        factors[c] = jnp.concatenate([step, step * out_f, step * out_b, in_f, in_b], axis=0).astype(BF16)
        scores = dot_nt(ctl[:, STATE : 2 * STATE], ctl[:, 0:STATE])
        scores_sc[c] = jnp.where(seg == seg_at(begin + lan), scores, 0.0)
        return carry_

    lax.fori_loop(0, CHUNKS, compact, 0)
    tot_sc[CHUNKS] = tot_sc[0] + tot_sc[1] + tot_sc[2] + tot_sc[3]
    log_recv[seq] = tot_sc[CHUNKS]

    def log_copy(k):
        peer = (seq + k) % NSEQ
        return remote(
            tot_sc.at[CHUNKS], log_recv.at[seq], s0_send.at[k], s0_recv.at[k], {"seq": peer}
        )

    def send_log(k, carry_):
        log_copy(k).start()
        return carry_

    lax.fori_loop(1, NSEQ, send_log, 0)

    def states_of(blk):
        spread_blk = spread_b[:, blk * COLS : (blk + 1) * COLS]

        def states(c, carry_):
            rows = pl.ds(pl.multiple_of(c * CHUNK, CHUNK), CHUNK)
            v = val[blk, rows, :].astype(F32)
            wide = dot(factors[c], spread_blk)
            wval[blk, rows, :] = (wide[0:CHUNK] * v).astype(BF16)
            weighted = jnp.concatenate(
                [wide[CHUNK : 2 * CHUNK] * v, wide[2 * CHUNK : 3 * CHUNK] * v], axis=1
            ).astype(BF16)
            reach[blk, 0, rows, :] = wide[3 * CHUNK : 4 * CHUNK].astype(BF16)
            reach[blk, 1, rows, :] = wide[4 * CHUNK : 5 * CHUNK].astype(BF16)
            chunk_state[blk * CHUNKS + c] = dot_tn(c_sc[rows, 0:STATE], weighted)
            return carry_

        lax.fori_loop(0, CHUNKS, states, 0)

    states_of(0)
    w_stage3(1)
    w_finish(0)
    project_values(1)
    states_of(1)

    spread_of = [spread[:, 0:COLS], spread[:, COLS:]]
    for blk in range(2):
        for c in range(CHUNKS):
            totx[blk, c] = jnp.exp2(exact(tot_sc[c], spread_of[blk]))
        f = chunk_state[blk * CHUNKS, :, 0:COLS]
        for c in range(1, CHUNKS):
            begin = base + c * CHUNK
            f = chunk_state[blk * CHUNKS + c, :, 0:COLS] + (
                totx[blk, c, 0:1, :] * keep_f(begin, begin + CHUNK - 1)
            ) * f
        b = chunk_state[blk * CHUNKS + CHUNKS - 1, :, COLS:]
        for c in range(CHUNKS - 2, -1, -1):
            begin = base + c * CHUNK
            b = chunk_state[blk * CHUNKS + c, :, COLS:] + (
                totx[blk, c, 0:1, :] * keep_b(begin, begin + CHUNK - 1)
            ) * b
        st_send[:, blk] = jnp.concatenate(
            [f.reshape(NSEQ, GROUP, COLS), b.reshape(NSEQ, GROUP, COLS)], axis=1
        ).astype(BF16)

    def state_copy(k):
        peer = (seq + k) % NSEQ
        return remote(
            st_send.at[peer], st_recv.at[seq], s1_send.at[k], s1_recv.at[k], {"seq": peer}
        )

    def send_state(k, carry_):
        state_copy(k).start()
        return carry_

    lax.fori_loop(1, NSEQ, send_state, 0)
    st_recv[seq] = st_send[seq]

    left = iota((CHUNK, 128), 1) < HEAD_DIM

    def within_of(blk):
        def within(c, carry_):
            rows = pl.ds(pl.multiple_of(c * CHUNK, CHUNK), CHUNK)
            scores = scores_sc[c]
            run = l_sc[blk, rows, :]
            before = e_sc[blk, rows, :]
            run_t = lt_sc[blk, c]
            before_t = et_sc[blk, c]
            for pair in range(PAIRS):
                fs, bs = [], []
                for h in (2 * pair, 2 * pair + 1):
                    gap = jnp.minimum(
                        run[:, h : h + 1] - run_t[h : h + 1, :],
                        before_t[h : h + 1, :] - before[:, h : h + 1],
                    )
                    g = (jnp.exp2(gap) * scores).astype(BF16)
                    fs.append(g * lower)
                    bs.append(g * upper)
                lhs = jnp.concatenate(
                    [jnp.concatenate(fs, axis=1), jnp.concatenate(bs, axis=1)], axis=0
                )
                lanes = slice(pair * 128, pair * 128 + 128)
                w = wval[blk, rows, lanes].astype(F32)
                rhs = jnp.concatenate([jnp.where(left, w, 0.0), jnp.where(left, 0.0, w)], axis=0)
                y = dot(lhs, rhs.astype(BF16))
                wide = slice(blk * COLS + pair * 128, blk * COLS + pair * 128 + 128)
                direct = skip_x[:, wide] * val[blk, rows, lanes].astype(F32)
                y_f[blk, rows, lanes] = y[0:CHUNK] + direct
                y_b[blk, rows, lanes] = y[CHUNK:] + direct
            return carry_

        lax.fori_loop(0, CHUNKS, within, 0)

    within_of(0)
    w_stage2(2)

    def await_log(k, carry_):
        src = (seq + NSEQ - k) % NSEQ
        remote(
            tot_sc.at[CHUNKS], log_recv.at[src], s0_send.at[k], s0_recv.at[k], {"seq": src}
        ).wait_recv()
        return carry_

    lax.fori_loop(1, NSEQ, await_log, 0)
    keep_x[...] = jnp.exp2(exact(log_recv[...].reshape(NSEQ * 8, 128), spread)).reshape(NSEQ, 8, 2 * COLS)

    def await_state(k, carry_):
        src = (seq + NSEQ - k) % NSEQ
        remote(
            st_send.at[src], st_recv.at[src], s1_send.at[k], s1_recv.at[k], {"seq": src}
        ).wait_recv()
        return carry_

    lax.fori_loop(1, NSEQ, await_state, 0)

    for blk in range(2):
        lanes = slice(blk * COLS, (blk + 1) * COLS)
        now = jnp.zeros((GROUP, COLS), F32)
        for d in range(NSEQ):
            enter[d, blk] = now
            if d < NSEQ - 1:
                begin = d * ROWS
                kept = keep_x[d, :, lanes] * keep_f(begin, begin + ROWS - 1)
                now = st_recv[d, blk].astype(F32)[0:GROUP] + kept * now
        now = jnp.zeros((GROUP, COLS), F32)
        for d in range(NSEQ - 1, -1, -1):
            en_send[d, blk] = jnp.concatenate([enter[d, blk], now], axis=0).astype(BF16)
            if d > 0:
                begin = d * ROWS
                kept = keep_x[d, :, lanes] * keep_b(begin, begin + ROWS - 1)
                now = st_recv[d, blk].astype(F32)[GROUP : 2 * GROUP] + kept * now

    def enter_copy(k):
        peer = (seq + k) % NSEQ
        return remote(
            en_send.at[peer], en_recv.at[seq], s2_send.at[k], s2_recv.at[k], {"seq": peer}
        )

    def send_enter(k, carry_):
        enter_copy(k).start()
        return carry_

    lax.fori_loop(1, NSEQ, send_enter, 0)
    en_recv[seq] = en_send[seq]
    w_stage3(2)

    within_of(1)

    g_copy.wait()
    project_gates(0)
    w_finish(1)
    project_gates(1)

    def await_enter(k, carry_):
        src = (seq + NSEQ - k) % NSEQ
        remote(
            en_send.at[src], en_recv.at[src], s2_send.at[k], s2_recv.at[k], {"seq": src}
        ).wait_recv()
        return carry_

    lax.fori_loop(1, NSEQ, await_enter, 0)

    for blk in range(2):
        both = en_recv[:, blk].astype(F32)
        f = both[:, 0:GROUP].reshape(STATE, COLS)
        b = both[:, GROUP : 2 * GROUP].reshape(STATE, COLS)
        for c in range(CHUNKS):
            rows = pl.ds(c * CHUNK, CHUNK)
            begin = base + c * CHUNK
            cc = c_sc[rows, STATE : 2 * STATE]
            y_f[blk, rows, :] += dot(cc, f.astype(BF16)) * reach[blk, 0, rows, :].astype(F32)
            if c < CHUNKS - 1:
                f = chunk_state[blk * CHUNKS + c, :, 0:COLS] + (
                    totx[blk, c, 0:1, :] * keep_f(begin, begin + CHUNK - 1)
                ) * f
        for c in range(CHUNKS - 1, -1, -1):
            rows = pl.ds(c * CHUNK, CHUNK)
            begin = base + c * CHUNK
            cc = c_sc[rows, STATE : 2 * STATE]
            y_b[blk, rows, :] += dot(cc, b.astype(BF16)) * reach[blk, 1, rows, :].astype(F32)
            if c > 0:
                b = chunk_state[blk * CHUNKS + c, :, COLS:] + (
                    totx[blk, c, 0:1, :] * keep_b(begin, begin + CHUNK - 1)
                ) * b

    ones = jnp.ones((8, COLS), BF16)
    row8 = iota((8, CHUNK), 0)

    def gate(c, carry_):
        rows = pl.ds(pl.multiple_of(c * CHUNK, CHUNK), CHUNK)
        sums = jnp.zeros((8, CHUNK), F32)
        for blk in range(2):
            a = act[blk, rows, :]
            for d, y in enumerate((y_f, y_b)):
                v = y[blk, rows, :] * a
                y[blk, rows, :] = v
                sq = v * v
                hi = sq.astype(BF16)
                lo = (sq - hi.astype(F32)).astype(BF16)
                sums = sums + jnp.where(row8 == d, dot_nt(ones, hi) + dot_nt(ones, lo), 0.0)
        ps_mine[:, rows] = sums
        return carry_

    lax.fori_loop(0, CHUNKS, gate, 0)
    for k, device in enumerate((to_d, to_n, to_o)):
        send(ps_mine, ps_buf.at[k], ps_send.at[k], ps_recv.at[k], device)
    w_finish(2)
    o_copy.wait()
    remote(ggain_ref, gg.at[1], ag_send.at[6], ag_recv.at[6], to_w).wait_recv()
    for k in range(3):
        remote(ps_mine, ps_buf.at[k], ps_send.at[k], ps_recv.at[k], to_n).wait_recv()
    sums = ps_mine[...] + ps_buf[0] + ps_buf[1] + ps_buf[2]
    scale = lax.rsqrt(sums * (1.0 / (COLS * NCHAN)) + norm_eps)
    scale = jnp.concatenate([scale, jnp.zeros((CHUNK - 8, ROWS), F32)], axis=0)
    for c in range(CHUNKS):
        rinv[c * CHUNK : (c + 1) * CHUNK, :] = scale[:, c * CHUNK : (c + 1) * CHUNK].T

    def combine(c, carry_):
        rows = pl.ds(pl.multiple_of(c * CHUNK, CHUNK), CHUNK)
        r = rinv[rows, :]
        for blk in range(2):
            both = y_f[blk, rows, :] * r[:, 0:1] + y_b[blk, rows, :] * r[:, 1:2]
            comb[rows, blk * COLS : (blk + 1) * COLS] = (both * gg[blk]).astype(BF16)
        return carry_

    lax.fori_loop(0, CHUNKS, combine, 0)

    def out_block(k):
        lanes = pl.ds(pl.multiple_of(k * COLS, COLS), COLS)

        def block(i, carry_):
            rows = pl.ds(pl.multiple_of(i * 256, 256), 256)
            part[k, rows, :] = (
                dot(comb[rows, 0:COLS], wo[0, :, lanes]) + dot(comb[rows, COLS:], wo[1, :, lanes])
            ).astype(BF16)
            return carry_

        lax.fori_loop(0, 2, block, 0)

    def rs(kind, src, dst, device):
        send(src, dst, rs_send.at[kind], rs_recv.at[kind], device)

    def rs_wait(kind, dst):
        remote(part.at[k_me, h1], dst, rs_send.at[kind], rs_recv.at[kind], to_n).wait_recv()

    def add(block, rows, ref):
        part[block, rows, :] = (part[block, rows, :].astype(F32) + ref[...].astype(F32)).astype(BF16)

    out_block(k_d)
    rs(0, part.at[k_d, h1], relay.at[0], to_o)
    rs(1, part.at[k_d, h2], relay.at[1], to_n)

    def out_second(i, carry_):
        out_block(jnp.where(i == 0, k_n, k_o))
        return carry_

    lax.fori_loop(0, 2, out_second, 0)
    rs(2, part.at[k_n, h2], rs_buf.at[0, h2], to_n)
    rs(4, part.at[k_o, h1], rs_buf.at[1, h1], to_o)
    out_block(k_me)
    rs_wait(0, relay.at[0])
    add(k_n, h1, relay.at[0])
    rs(3, part.at[k_n, h1], rs_buf.at[0, h1], to_n)
    rs_wait(1, relay.at[1])
    add(k_o, h2, relay.at[1])
    rs(5, part.at[k_o, h2], rs_buf.at[1, h2], to_o)

    def finish(i, rows):
        total = part[k_me, rows, :].astype(F32) + rs_buf[0, rows, :].astype(F32) + rs_buf[1, rows, :].astype(F32)
        out_ref[rows, :] = dot(total.astype(BF16), flip).astype(BF16)

    rs_wait(4, rs_buf.at[1, h1])
    rs_wait(2, rs_buf.at[0, h2])
    rs_wait(3, rs_buf.at[0, h1])
    finish(0, h1)
    rs_wait(5, rs_buf.at[1, h2])
    finish(1, h2)

    for copy in started:
        copy.wait_send()

    def sent_seq(k, carry_):
        log_copy(k).wait_send()
        state_copy(k).wait_send()
        enter_copy(k).wait_send()
        return carry_

    lax.fori_loop(1, NSEQ, sent_seq, 0)


def local(
    hidden, norm_gain, w_values, w_gates, w_control, dt_bias, decay_total, skip_gain, gate_gain, w_out, doc_starts
):
    vmem = pl.BlockSpec(memory_space=pltpu.VMEM)
    hbm = pl.BlockSpec(memory_space=pl.ANY)
    smem = pl.BlockSpec(memory_space=pltpu.SMEM)
    dma = pltpu.SemaphoreType.DMA
    scratch = [
        pltpu.VMEM((ROWS, COLS), BF16),
        pltpu.VMEM((2, HALF, COLS), BF16),
        pltpu.VMEM((2, HALF, COLS), BF16),
        pltpu.VMEM((CTRL, HALF), BF16),
        pltpu.VMEM((2, COLS, HALF), BF16),
        pltpu.VMEM((2, 1, COLS), F32),
        pltpu.VMEM((4, ROWS, COLS), BF16),
        pltpu.VMEM((ROWS, HALF), BF16),
        pltpu.VMEM((ROWS, 128), F32),
        pltpu.VMEM((ROWS, 128), F32),
        pltpu.VMEM((ROWS, CTRL), BF16),
        pltpu.VMEM((CHUNKS, 5 * CHUNK, 128), BF16),
        pltpu.VMEM((CHUNKS, CHUNK, CHUNK), F32),
        pltpu.VMEM((2, ROWS, 128), F32),
        pltpu.VMEM((2, ROWS, 128), F32),
        pltpu.VMEM((2, CHUNKS, 8, 128), F32),
        pltpu.VMEM((2, CHUNKS, 8, 128), F32),
        pltpu.VMEM((2, ROWS, COLS), BF16),
        pltpu.VMEM((2, ROWS, COLS), BF16),
        pltpu.VMEM((2, ROWS, COLS), F32),
        pltpu.VMEM((2, 2, ROWS, COLS), BF16),
        pltpu.VMEM((2 * CHUNKS, STATE, 2 * COLS), F32),
        pltpu.VMEM((CHUNKS + 1, 8, 128), F32),
        pltpu.VMEM((2, CHUNKS, 8, COLS), F32),
        pltpu.VMEM((NSEQ, 8, 128), F32),
        pltpu.VMEM((NSEQ, 8, 2 * COLS), F32),
        pltpu.VMEM((NSEQ, 2, 2 * GROUP, COLS), BF16),
        pltpu.VMEM((NSEQ, 2, 2 * GROUP, COLS), BF16),
        pltpu.VMEM((NSEQ, 2, GROUP, COLS), F32),
        pltpu.VMEM((NSEQ, 2, 2 * GROUP, COLS), BF16),
        pltpu.VMEM((NSEQ, 2, 2 * GROUP, COLS), BF16),
        pltpu.VMEM((2, ROWS, COLS), F32),
        pltpu.VMEM((2, ROWS, COLS), F32),
        pltpu.VMEM((3, 8, ROWS), F32),
        pltpu.VMEM((8, ROWS), F32),
        pltpu.VMEM((ROWS, 2 * COLS), BF16),
        pltpu.VMEM((4, ROWS, COLS), BF16),
        pltpu.VMEM((2, ROWS, COLS), BF16),
        pltpu.VMEM((2, HALF_ROWS, COLS), BF16),
        dma((5,)),
        dma((7,)),
        dma((7,)),
        dma((3, 10)),
        dma((3, 10)),
        dma((NSEQ,)),
        dma((NSEQ,)),
        dma((NSEQ,)),
        dma((NSEQ,)),
        dma((NSEQ,)),
        dma((NSEQ,)),
        dma((3,)),
        dma((3,)),
        dma((6,)),
        dma((6,)),
    ]
    return pl.pallas_call(
        kernel,
        name="mixer",
        out_shape=jax.ShapeDtypeStruct((ROWS, COLS), BF16),
        in_specs=[hbm, vmem, hbm, hbm, hbm, vmem, vmem, vmem, vmem, hbm, smem],
        out_specs=vmem,
        scratch_shapes=scratch,
        compiler_params=pltpu.CompilerParams(
            collective_id=0, has_side_effects=True, vmem_limit_bytes=56 * 2**20
        ),
    )(
        hidden,
        norm_gain.reshape(4, 1, COLS),
        w_values,
        w_gates,
        w_control.T,
        dt_bias.reshape(1, HEADS),
        decay_total.reshape(1, HEADS),
        skip_gain.reshape(1, HEADS),
        gate_gain.reshape(1, COLS),
        w_out,
        doc_starts,
    )


def solution(mesh):
    in_specs = (
        P("seq", "chan"),
        P(),
        P(None, "chan"),
        P(None, "chan"),
        P(),
        P(),
        P(),
        P(),
        P("chan"),
        P("chan", None),
        P(),
    )
    return jax.shard_map(local, mesh=mesh, in_specs=in_specs, out_specs=P("seq", "chan"), check_vma=False)
```

```python
import jax
import jax.numpy as jnp
from jax import lax
from jax.experimental import pallas as pl
from jax.experimental.pallas import tpu as pltpu
from jax.sharding import PartitionSpec as P

MESH = pl.DeviceIdType.MESH
F32 = jnp.float32
BF16 = jnp.bfloat16
HIGHEST = lax.Precision.HIGHEST

HEAD_DIM = 64
STATE = 128
CHUNK = 128
ROWS = 512
COLS = 512
HALF = 2048
HEADS = 64
NCHAN = 8
NSEQ = 16
CHUNKS = ROWS // CHUNK
PAIRS = COLS // 128
BLOCK_HEADS = COLS // HEAD_DIM
GROUP = STATE // NSEQ
HALF_ROWS = ROWS // 2
CTRL = 2 * STATE + HEADS
LOG2E = 1.4426950408889634
norm_eps = 1e-05


def dot(a, b):
    return jnp.dot(a, b, preferred_element_type=F32)


def dot_nt(a, b):
    return lax.dot_general(a, b, (((1,), (1,)), ((), ())), preferred_element_type=F32)


def dot_tn(a, b):
    return lax.dot_general(a, b, (((0,), (0,)), ((), ())), preferred_element_type=F32)


def exact(rows, table):
    return jnp.dot(rows, table, precision=HIGHEST, preferred_element_type=F32)


def iota(shape, dim):
    return lax.broadcasted_iota(jnp.int32, shape, dim)


def remote(src, dst, send_sem, recv_sem, device):
    return pltpu.make_async_remote_copy(
        src_ref=src,
        dst_ref=dst,
        send_sem=send_sem,
        recv_sem=recv_sem,
        device_id=device,
        device_id_type=MESH,
    )


def kernel(
    x_hbm, gain_ref, wv_hbm, wg_hbm, wc_hbm, bias_ref, decay_ref, skip_ref, ggain_ref, wo_hbm, docs,
    out_ref,
    x_v, wv, wg, wc, wo, gg, gath, xg, sumsq, rinv,
    c_sc, factors, scores_sc, l_sc, e_sc, lt_sc, et_sc, wval, val, act, reach, chunk_state, tot_sc, totx,
    log_recv, keep_x, st_send, st_recv, enter, en_send, en_recv, y_f, y_b,
    ps_buf, ps_mine, comb, part, rs_buf, relay,
    loc_sem, ag_send, ag_recv, w_send, w_recv, s0_send, s0_recv, s1_send, s1_recv, s2_send, s2_recv,
    ps_send, ps_recv, rs_send, rs_recv,
):
    seq = lax.axis_index("seq")
    chan = lax.axis_index("chan")
    yy = chan // 2
    zz = chan % 2
    y_near = yy + 1 - 2 * (yy % 2)
    c_n = y_near * 2 + zz
    c_o = yy * 2 + 1 - zz
    c_d = y_near * 2 + 1 - zz
    c_w = (3 - yy) * 2 + zz
    mirrored = chan >= 4

    def block_of(c):
        return jnp.where(mirrored, 7 - c, c)

    k_me, k_n, k_o, k_d = block_of(chan), block_of(c_n), block_of(c_o), block_of(c_d)
    to_n, to_o, to_d, to_w = {"chan": c_n}, {"chan": c_o}, {"chan": c_d}, {"chan": c_w}
    to_right, to_left = {"seq": (seq + 4) % NSEQ}, {"seq": (seq + 12) % NSEQ}
    to_twin = {"seq": seq + 1 - 2 * (seq % 2)}
    q_me = (seq // 4) * 2 + seq % 2
    q_twin = (seq // 4) * 2 + 1 - seq % 2

    barrier = pltpu.get_barrier_semaphore()
    for device in (to_n, to_o, to_d, to_w):
        pl.semaphore_signal(barrier, inc=1, device_id=device, device_id_type=MESH)

    def greet_seq(k, carry_):
        pl.semaphore_signal(barrier, inc=1, device_id={"seq": (seq + k) % NSEQ}, device_id_type=MESH)
        return carry_

    lax.fori_loop(1, NSEQ, greet_seq, 0)

    x_copy = pltpu.make_async_copy(x_hbm, x_v, loc_sem.at[0])
    x_copy.start()
    v_copy = pltpu.make_async_copy(wv_hbm, wv.at[0], loc_sem.at[1])
    c_copy = pltpu.make_async_copy(wc_hbm, wc, loc_sem.at[2])
    g_copy = pltpu.make_async_copy(wg_hbm, wg.at[0], loc_sem.at[3])
    o_copy = pltpu.make_async_copy(wo_hbm, wo.at[pl.ds(0, COLS)], loc_sem.at[4])

    col = iota((COLS, COLS), 1)
    wanted = jnp.where(mirrored, COLS - 1 - col, col)
    flip = jnp.where(iota((COLS, COLS), 0) == wanted, 1.0, 0.0).astype(BF16)
    x_copy.wait()
    gath[k_me] = dot(x_v[...], flip).astype(BF16)
    gg[0] = ggain_ref[...]

    pl.semaphore_wait(barrier, 4 + NSEQ - 1)

    h1, h2 = pl.ds(0, HALF_ROWS), pl.ds(HALF_ROWS, HALF_ROWS)
    whole = pl.ds(0, ROWS)
    started = []

    def send(src, dst, send_sem, recv_sem, device):
        copy = remote(src, dst, send_sem, recv_sem, device)
        copy.start()
        started.append(copy)

    def ag(kind, block, rows, device):
        ref = gath.at[block, rows]
        send(ref, ref, ag_send.at[kind], ag_recv.at[kind], device)

    def ag_wait(kind, block, rows):
        ref = gath.at[block, rows]
        remote(ref, ref, ag_send.at[kind], ag_recv.at[kind], to_n).wait_recv()

    tensors = ((wv_hbm, wv, HALF // 8), (wg_hbm, wg, HALF // 8))

    def w_rows(t, dx, twin, half):
        size = tensors[t][2]
        q = ((q_twin if twin else q_me) + 2 * dx) % 8
        if half is None:
            return pl.ds(pl.multiple_of(q * size, size), size)
        return pl.ds(pl.multiple_of(q * size + half * (size // 2), size // 2), size // 2)

    def w_from_partner(t):
        hbm, buf, _ = tensors[t]
        rows = w_rows(t, 0, False, None)
        send(hbm.at[rows], buf.at[1, rows], w_send.at[t, 0], w_recv.at[t, 0], to_w)

    def w_on(t, kind, dx, half, device):
        ref = tensors[t][1].at[1, w_rows(t, dx, False, half)]
        send(ref, ref, w_send.at[t, kind], w_recv.at[t, kind], device)

    def w_wait(t, kind, dx, twin, half):
        ref = tensors[t][1].at[1, w_rows(t, dx, twin, half)]
        remote(ref, ref, w_send.at[t, kind], w_recv.at[t, kind], to_w).wait_recv()

    def w_stage1(t):
        w_wait(t, 0, 0, False, None)
        w_on(t, 1, 0, None, to_right)
        w_on(t, 2, 0, None, to_left)
        w_on(t, 3, 0, None, to_twin)

    def w_stage2(t):
        w_wait(t, 1, 3, False, None)
        w_on(t, 4, 3, 0, to_right)
        w_on(t, 5, 3, None, to_twin)
        w_wait(t, 2, 1, False, None)
        w_on(t, 6, 1, 1, to_left)
        w_on(t, 7, 1, None, to_twin)

    def w_stage3(t):
        w_wait(t, 4, 2, False, 0)
        w_on(t, 8, 2, 0, to_twin)
        w_wait(t, 6, 2, False, 1)
        w_on(t, 9, 2, 1, to_twin)

    def wo_rows(core, block):
        return pl.ds(pl.multiple_of(block * COLS + core * HALF_ROWS, HALF_ROWS), HALF_ROWS)

    core = seq % 2

    def wo_from_partner():
        send(wo_hbm.at[wo_rows(core, 0)], wo.at[wo_rows(core, 1)], w_send.at[2, 0], w_recv.at[2, 0], to_w)

    def wo_to_twin():
        ref = wo.at[wo_rows(core, 1)]
        remote(ref, ref, w_send.at[2, 0], w_recv.at[2, 0], to_w).wait_recv()
        send(ref, ref, w_send.at[2, 1], w_recv.at[2, 1], to_twin)

    def wo_finish():
        ref = wo.at[wo_rows(1 - core, 1)]
        remote(ref, ref, w_send.at[2, 1], w_recv.at[2, 1], to_w).wait_recv()

    def w_finish(t):
        w_wait(t, 3, 0, True, None)
        w_wait(t, 5, 3, True, None)
        w_wait(t, 7, 1, True, None)
        w_wait(t, 8, 2, True, 0)
        w_wait(t, 9, 2, True, 1)

    ag(0, k_me, h1, to_n)
    ag(2, k_me, h2, to_o)
    w_from_partner(0)
    ag(1, k_me, h2, to_n)
    ag(3, k_me, h1, to_o)
    w_from_partner(1)
    send(ggain_ref, gg.at[1], ag_send.at[6], ag_recv.at[6], to_w)
    for copy in (v_copy, c_copy, g_copy, o_copy):
        copy.start()

    def scale_block(k):
        gain = gain_ref[k]
        lanes = pl.ds(pl.multiple_of(k * COLS, COLS), COLS)

        def scale_rows(i, carry_):
            rows = pl.ds(pl.multiple_of(i * 64, 64), 64)
            x = gath[k, rows, :].astype(F32)
            xg[rows, lanes] = (x * gain).astype(BF16)
            sq = x * x
            sumsq[rows, :] += sq[:, 0:128] + sq[:, 128:256] + sq[:, 256:384] + sq[:, 384:512]
            return carry_

        lax.fori_loop(0, ROWS // 64, scale_rows, 0)

    sumsq[...] = jnp.zeros_like(sumsq)
    scale_block(k_me)

    lane = iota((HEADS, 128), 1)
    head = iota((HEADS, 128), 0)
    picked = ((head == chan * BLOCK_HEADS + lane) & (lane < BLOCK_HEADS)) | (
        (head == (c_w - 1) * BLOCK_HEADS + lane) & (lane >= BLOCK_HEADS) & (lane < 2 * BLOCK_HEADS)
    )
    pick = jnp.where(picked, 1.0, 0.0)
    spread = jnp.where(iota((128, 2 * COLS), 0) == iota((128, 2 * COLS), 1) // HEAD_DIM, 1.0, 0.0)
    pick_b = pick.astype(BF16)
    spread_b = spread.astype(BF16)

    def head_row(ref):
        return exact(jnp.broadcast_to(ref[...], (8, HEADS)), pick)

    bias = head_row(bias_ref)[0:1]
    slope = head_row(decay_ref)[0:1] * (-LOG2E / (ROWS * NSEQ))
    skip_x = exact(head_row(skip_ref), spread)[0:1]

    starts = [docs[k] for k in range(4)]
    base = seq * ROWS

    def seg_at(position):
        total = jnp.int32(0)
        for start in starts:
            total = total + jnp.where(position >= start, 1, 0)
        return total

    def same(a, b):
        return jnp.where(seg_at(a) == seg_at(b), 1.0, 0.0)

    def keep_f(begin, end):
        return same(end, begin - 1)

    def keep_b(begin, end):
        return same(begin, end + 1)

    sub = iota((CHUNK, CHUNK), 0)
    lan = iota((CHUNK, CHUNK), 1)
    lower = jnp.where(sub >= lan, 1.0, 0.0).astype(BF16)
    upper = jnp.where(sub <= lan, 1.0, 0.0).astype(BF16)

    ag_wait(0, k_n, h1)
    ag(4, k_n, h1, to_o)
    ag_wait(2, k_o, h2)
    ag(5, k_o, h2, to_n)
    w_stage1(0)
    ag_wait(1, k_n, h2)
    scale_block(k_n)
    ag_wait(3, k_o, h1)
    scale_block(k_o)
    w_stage2(0)
    w_stage3(0)
    w_stage1(1)
    wo_from_partner()
    ag_wait(4, k_d, h1)
    ag_wait(5, k_d, h2)
    scale_block(k_d)

    for i in range(CHUNKS):
        rows = pl.ds(i * CHUNK, CHUNK)
        total = jnp.sum(sumsq[rows, :], axis=1, keepdims=True)
        rinv[rows, :] = jnp.broadcast_to(lax.rsqrt(total * (1.0 / HALF) + norm_eps), (CHUNK, 128))

    def project_control(i, carry_):
        rows = pl.ds(pl.multiple_of(i * 256, 256), 256)
        c_sc[rows, :] = (dot_nt(xg[rows, :], wc[...]) * rinv[rows, :][:, 0:1]).astype(BF16)
        return carry_

    def project_values(blk):
        def go(i, carry_):
            rows = pl.ds(pl.multiple_of(i * 256, 256), 256)
            val[blk, rows, :] = (dot(xg[rows, :], wv[blk]) * rinv[rows, :][:, 0:1]).astype(BF16)
            return carry_

        lax.fori_loop(0, 2, go, 0)

    def project_gates(blk):
        def go(i, carry_):
            rows = pl.ds(pl.multiple_of(i * 256, 256), 256)
            g = (dot(xg[rows, :], wg[blk]) * rinv[rows, :][:, 0:1]).astype(BF16).astype(F32)
            act[blk, rows, :] = g / (1.0 + jnp.exp(-g))
            return carry_

        lax.fori_loop(0, 2, go, 0)

    c_copy.wait()
    lax.fori_loop(0, 2, project_control, 0)
    v_copy.wait()
    project_values(0)

    def compact(c, carry_):
        rows = pl.ds(pl.multiple_of(c * CHUNK, CHUNK), CHUNK)
        begin = base + c * CHUNK
        end = begin + CHUNK - 1
        ctl = c_sc[rows, :]
        z = dot(ctl[:, 2 * STATE :], pick_b) + bias
        step = jnp.maximum(z, 0.0) + jnp.log1p(jnp.exp(-jnp.abs(z)))
        log_rate = slope * step
        p1 = log_rate.astype(BF16)
        rest = log_rate - p1.astype(F32)
        p2 = rest.astype(BF16)
        p3 = (rest - p2.astype(F32)).astype(BF16)
        run = dot(lower, p1) + dot(lower, p2) + dot(lower, p3)
        before = run - log_rate
        total = run[CHUNK - 1 : CHUNK, :]
        l_sc[0, rows, :] = run
        e_sc[0, rows, :] = before
        l_sc[1, rows, :] = pltpu.roll(run, 128 - BLOCK_HEADS, 1)
        e_sc[1, rows, :] = pltpu.roll(before, 128 - BLOCK_HEADS, 1)
        run_t = run.T
        before_t = before.T
        for blk in range(2):
            lt_sc[blk, c] = run_t[blk * BLOCK_HEADS : (blk + 1) * BLOCK_HEADS, :]
            et_sc[blk, c] = before_t[blk * BLOCK_HEADS : (blk + 1) * BLOCK_HEADS, :]
        tot_sc[c] = jnp.broadcast_to(total, (8, 128))
        seg = seg_at(begin + sub)

        def mask(position):
            return jnp.where(seg == seg_at(position), 1.0, 0.0)

        out_f = jnp.exp2(total - run) * mask(end)
        out_b = jnp.exp2(before) * mask(begin)
        in_f = jnp.exp2(run) * mask(begin - 1)
        in_b = jnp.exp2(total - before) * mask(end + 1)
        factors[c] = jnp.concatenate([step, step * out_f, step * out_b, in_f, in_b], axis=0).astype(BF16)
        scores = dot_nt(ctl[:, STATE : 2 * STATE], ctl[:, 0:STATE])
        scores_sc[c] = jnp.where(seg == seg_at(begin + lan), scores, 0.0)
        return carry_

    lax.fori_loop(0, CHUNKS, compact, 0)
    tot_sc[CHUNKS] = tot_sc[0] + tot_sc[1] + tot_sc[2] + tot_sc[3]
    log_recv[seq] = tot_sc[CHUNKS]

    def log_copy(k):
        peer = (seq + k) % NSEQ
        return remote(
            tot_sc.at[CHUNKS], log_recv.at[seq], s0_send.at[k], s0_recv.at[k], {"seq": peer}
        )

    def send_log(k, carry_):
        log_copy(k).start()
        return carry_

    lax.fori_loop(1, NSEQ, send_log, 0)

    def states_of(blk):
        spread_blk = spread_b[:, blk * COLS : (blk + 1) * COLS]

        def states(c, carry_):
            rows = pl.ds(pl.multiple_of(c * CHUNK, CHUNK), CHUNK)
            v = val[blk, rows, :].astype(F32)
            wide = dot(factors[c], spread_blk)
            wval[blk, rows, :] = (wide[0:CHUNK] * v).astype(BF16)
            weighted = jnp.concatenate(
                [wide[CHUNK : 2 * CHUNK] * v, wide[2 * CHUNK : 3 * CHUNK] * v], axis=1
            ).astype(BF16)
            reach[blk, 0, rows, :] = wide[3 * CHUNK : 4 * CHUNK].astype(BF16)
            reach[blk, 1, rows, :] = wide[4 * CHUNK : 5 * CHUNK].astype(BF16)
            chunk_state[blk * CHUNKS + c] = dot_tn(c_sc[rows, 0:STATE], weighted)
            return carry_

        lax.fori_loop(0, CHUNKS, states, 0)

    spread_of = [spread[:, 0:COLS], spread[:, COLS:]]

    def leave(blk):
        for c in range(CHUNKS):
            totx[blk, c] = jnp.exp2(exact(tot_sc[c], spread_of[blk]))
        f = chunk_state[blk * CHUNKS, :, 0:COLS]
        for c in range(1, CHUNKS):
            begin = base + c * CHUNK
            f = chunk_state[blk * CHUNKS + c, :, 0:COLS] + (
                totx[blk, c, 0:1, :] * keep_f(begin, begin + CHUNK - 1)
            ) * f
        b = chunk_state[blk * CHUNKS + CHUNKS - 1, :, COLS:]
        for c in range(CHUNKS - 2, -1, -1):
            begin = base + c * CHUNK
            b = chunk_state[blk * CHUNKS + c, :, COLS:] + (
                totx[blk, c, 0:1, :] * keep_b(begin, begin + CHUNK - 1)
            ) * b
        st_send[blk] = jnp.concatenate(
            [f.reshape(NSEQ, GROUP, COLS), b.reshape(NSEQ, GROUP, COLS)], axis=1
        ).astype(BF16)

        def send_state(k, carry_):
            state_copy(blk, k).start()
            return carry_

        lax.fori_loop(1, NSEQ, send_state, 0)
        st_recv[blk, seq] = st_send[blk, seq]

    def state_copy(blk, k):
        peer = (seq + k) % NSEQ
        return remote(
            st_send.at[blk, peer], st_recv.at[blk, seq], s1_send.at[blk, k], s1_recv.at[blk, k], {"seq": peer}
        )

    states_of(0)
    leave(0)
    w_finish(0)
    project_values(1)
    w_stage2(1)
    states_of(1)
    leave(1)
    w_stage3(1)

    left = iota((CHUNK, 128), 1) < HEAD_DIM

    def within_of(blk):
        def within(c, carry_):
            rows = pl.ds(pl.multiple_of(c * CHUNK, CHUNK), CHUNK)
            scores = scores_sc[c]
            run = l_sc[blk, rows, :]
            before = e_sc[blk, rows, :]
            run_t = lt_sc[blk, c]
            before_t = et_sc[blk, c]
            for pair in range(PAIRS):
                fs, bs = [], []
                for h in (2 * pair, 2 * pair + 1):
                    gap = jnp.minimum(
                        run[:, h : h + 1] - run_t[h : h + 1, :],
                        before_t[h : h + 1, :] - before[:, h : h + 1],
                    )
                    g = (jnp.exp2(gap) * scores).astype(BF16)
                    fs.append(g * lower)
                    bs.append(g * upper)
                lhs = jnp.concatenate(
                    [jnp.concatenate(fs, axis=1), jnp.concatenate(bs, axis=1)], axis=0
                )
                lanes = slice(pair * 128, pair * 128 + 128)
                w = wval[blk, rows, lanes].astype(F32)
                rhs = jnp.concatenate([jnp.where(left, w, 0.0), jnp.where(left, 0.0, w)], axis=0)
                y = dot(lhs, rhs.astype(BF16))
                wide = slice(blk * COLS + pair * 128, blk * COLS + pair * 128 + 128)
                direct = skip_x[:, wide] * val[blk, rows, lanes].astype(F32)
                y_f[blk, rows, lanes] = y[0:CHUNK] + direct
                y_b[blk, rows, lanes] = y[CHUNK:] + direct
            return carry_

        lax.fori_loop(0, CHUNKS, within, 0)

    def await_log(k, carry_):
        src = (seq + NSEQ - k) % NSEQ
        remote(
            tot_sc.at[CHUNKS], log_recv.at[src], s0_send.at[k], s0_recv.at[k], {"seq": src}
        ).wait_recv()
        return carry_

    def scan_devices(blk):
        def await_state(k, carry_):
            src = (seq + NSEQ - k) % NSEQ
            remote(
                st_send.at[blk, src], st_recv.at[blk, src], s1_send.at[blk, k], s1_recv.at[blk, k], {"seq": src}
            ).wait_recv()
            return carry_

        lax.fori_loop(1, NSEQ, await_state, 0)
        lanes = slice(blk * COLS, (blk + 1) * COLS)
        now = jnp.zeros((GROUP, COLS), F32)
        for d in range(NSEQ):
            enter[d, blk] = now
            if d < NSEQ - 1:
                begin = d * ROWS
                kept = keep_x[d, :, lanes] * keep_f(begin, begin + ROWS - 1)
                now = st_recv[blk, d].astype(F32)[0:GROUP] + kept * now
        now = jnp.zeros((GROUP, COLS), F32)
        for d in range(NSEQ - 1, -1, -1):
            en_send[blk, d] = jnp.concatenate([enter[d, blk], now], axis=0).astype(BF16)
            if d > 0:
                begin = d * ROWS
                kept = keep_x[d, :, lanes] * keep_b(begin, begin + ROWS - 1)
                now = st_recv[blk, d].astype(F32)[GROUP : 2 * GROUP] + kept * now

        def send_enter(k, carry_):
            enter_copy(blk, k).start()
            return carry_

        lax.fori_loop(1, NSEQ, send_enter, 0)
        en_recv[blk, seq] = en_send[blk, seq]

    def enter_copy(blk, k):
        peer = (seq + k) % NSEQ
        return remote(
            en_send.at[blk, peer], en_recv.at[blk, seq], s2_send.at[blk, k], s2_recv.at[blk, k], {"seq": peer}
        )

    lax.fori_loop(1, NSEQ, await_log, 0)
    keep_x[...] = jnp.exp2(exact(log_recv[...].reshape(NSEQ * 8, 128), spread)).reshape(NSEQ, 8, 2 * COLS)
    scan_devices(0)
    within_of(0)
    scan_devices(1)
    wo_to_twin()
    within_of(1)
    g_copy.wait()
    project_gates(0)
    w_finish(1)
    project_gates(1)

    def outside(blk):
        def await_enter(k, carry_):
            src = (seq + NSEQ - k) % NSEQ
            remote(
                en_send.at[blk, src], en_recv.at[blk, src], s2_send.at[blk, k], s2_recv.at[blk, k], {"seq": src}
            ).wait_recv()
            return carry_

        lax.fori_loop(1, NSEQ, await_enter, 0)
        both = en_recv[blk].astype(F32)
        f = both[:, 0:GROUP].reshape(STATE, COLS)
        b = both[:, GROUP : 2 * GROUP].reshape(STATE, COLS)
        for c in range(CHUNKS):
            rows = pl.ds(c * CHUNK, CHUNK)
            begin = base + c * CHUNK
            cc = c_sc[rows, STATE : 2 * STATE]
            y_f[blk, rows, :] += dot(cc, f.astype(BF16)) * reach[blk, 0, rows, :].astype(F32)
            if c < CHUNKS - 1:
                f = chunk_state[blk * CHUNKS + c, :, 0:COLS] + (
                    totx[blk, c, 0:1, :] * keep_f(begin, begin + CHUNK - 1)
                ) * f
        for c in range(CHUNKS - 1, -1, -1):
            rows = pl.ds(c * CHUNK, CHUNK)
            begin = base + c * CHUNK
            cc = c_sc[rows, STATE : 2 * STATE]
            y_b[blk, rows, :] += dot(cc, b.astype(BF16)) * reach[blk, 1, rows, :].astype(F32)
            if c > 0:
                b = chunk_state[blk * CHUNKS + c, :, COLS:] + (
                    totx[blk, c, 0:1, :] * keep_b(begin, begin + CHUNK - 1)
                ) * b

    outside(0)
    outside(1)

    ones = jnp.ones((8, COLS), BF16)
    row8 = iota((8, CHUNK), 0)

    def gate(c, carry_):
        rows = pl.ds(pl.multiple_of(c * CHUNK, CHUNK), CHUNK)
        sums = jnp.zeros((8, CHUNK), F32)
        for blk in range(2):
            a = act[blk, rows, :]
            for d, y in enumerate((y_f, y_b)):
                v = y[blk, rows, :] * a
                y[blk, rows, :] = v
                sq = v * v
                hi = sq.astype(BF16)
                lo = (sq - hi.astype(F32)).astype(BF16)
                sums = sums + jnp.where(row8 == d, dot_nt(ones, hi) + dot_nt(ones, lo), 0.0)
        ps_mine[c // 2, :, pl.ds(pl.multiple_of((c % 2) * CHUNK, CHUNK), CHUNK)] = sums
        return carry_

    def send_sums(half):
        for k, device in enumerate((to_d, to_n, to_o)):
            send(ps_mine.at[half], ps_buf.at[half, k], ps_send.at[half, k], ps_recv.at[half, k], device)

    def norm_half(half):
        for k in range(3):
            remote(
                ps_mine.at[half], ps_buf.at[half, k], ps_send.at[half, k], ps_recv.at[half, k], to_n
            ).wait_recv()
        sums = ps_mine[half] + ps_buf[half, 0] + ps_buf[half, 1] + ps_buf[half, 2]
        scale = lax.rsqrt(sums * (1.0 / (COLS * NCHAN)) + norm_eps)
        scale = jnp.concatenate([scale, jnp.zeros((CHUNK - 8, HALF_ROWS), F32)], axis=0)
        for i in range(2):
            c = 2 * half + i
            rows = slice(c * CHUNK, (c + 1) * CHUNK)
            r = scale[:, i * CHUNK : (i + 1) * CHUNK].T
            for blk in range(2):
                both = y_f[blk, rows, :] * r[:, 0:1] + y_b[blk, rows, :] * r[:, 1:2]
                comb[rows, blk * COLS : (blk + 1) * COLS] = (both * gg[blk]).astype(BF16)

    lax.fori_loop(0, 2, gate, 0)
    send_sums(0)
    lax.fori_loop(2, 4, gate, 0)
    send_sums(1)
    wo_finish()
    o_copy.wait()
    remote(ggain_ref, gg.at[1], ag_send.at[6], ag_recv.at[6], to_w).wait_recv()

    def out_block(k, half):
        lanes = pl.ds(pl.multiple_of(k * COLS, COLS), COLS)
        rows = pl.ds(half * HALF_ROWS, HALF_ROWS)
        part[k, rows, :] = dot(comb[rows, :], wo[:, lanes]).astype(BF16)

    def quarter(half, i):
        return pl.ds((2 * half + i) * CHUNK, CHUNK)

    def rs(half, kind, src, dst, device):
        send(src, dst, rs_send.at[half, kind], rs_recv.at[half, kind], device)

    def rs_wait(half, kind, dst):
        remote(
            part.at[k_me, quarter(0, 0)], dst, rs_send.at[half, kind], rs_recv.at[half, kind], to_n
        ).wait_recv()

    def add(block, rows, ref):
        part[block, rows, :] = (part[block, rows, :].astype(F32) + ref[...].astype(F32)).astype(BF16)

    def produce(half):
        q1, q2 = quarter(half, 0), quarter(half, 1)
        out_block(k_d, half)
        rs(half, 0, part.at[k_d, q1], relay.at[half, 0], to_o)
        rs(half, 1, part.at[k_d, q2], relay.at[half, 1], to_n)
        out_block(k_n, half)
        rs(half, 2, part.at[k_n, q2], rs_buf.at[0, q2], to_n)
        out_block(k_o, half)
        rs(half, 4, part.at[k_o, q1], rs_buf.at[1, q1], to_o)

    def hand_on(half):
        q1, q2 = quarter(half, 0), quarter(half, 1)
        rs_wait(half, 0, relay.at[half, 0])
        add(k_n, q1, relay.at[half, 0])
        rs(half, 3, part.at[k_n, q1], rs_buf.at[0, q1], to_n)
        rs_wait(half, 1, relay.at[half, 1])
        add(k_o, q2, relay.at[half, 1])
        rs(half, 5, part.at[k_o, q2], rs_buf.at[1, q2], to_o)

    def finish(half):
        q1, q2 = quarter(half, 0), quarter(half, 1)
        rs_wait(half, 4, rs_buf.at[1, q1])
        rs_wait(half, 2, rs_buf.at[0, q2])
        rs_wait(half, 3, rs_buf.at[0, q1])
        rs_wait(half, 5, rs_buf.at[1, q2])
        rows = pl.ds(half * HALF_ROWS, HALF_ROWS)
        total = part[k_me, rows, :].astype(F32) + rs_buf[0, rows, :].astype(F32) + rs_buf[1, rows, :].astype(F32)
        out_ref[rows, :] = dot(total.astype(BF16), flip).astype(BF16)

    norm_half(0)
    produce(0)
    norm_half(1)
    hand_on(0)
    produce(1)
    out_block(k_me, 0)
    out_block(k_me, 1)
    hand_on(1)
    finish(0)
    finish(1)

    for copy in started:
        copy.wait_send()

    def sent_seq(k, carry_):
        log_copy(k).wait_send()
        for blk in range(2):
            state_copy(blk, k).wait_send()
            enter_copy(blk, k).wait_send()
        return carry_

    lax.fori_loop(1, NSEQ, sent_seq, 0)


def local(
    hidden, norm_gain, w_values, w_gates, w_control, dt_bias, decay_total, skip_gain, gate_gain, w_out, doc_starts
):
    vmem = pl.BlockSpec(memory_space=pltpu.VMEM)
    hbm = pl.BlockSpec(memory_space=pl.ANY)
    smem = pl.BlockSpec(memory_space=pltpu.SMEM)
    dma = pltpu.SemaphoreType.DMA
    scratch = [
        pltpu.VMEM((ROWS, COLS), BF16),
        pltpu.VMEM((2, HALF, COLS), BF16),
        pltpu.VMEM((2, HALF, COLS), BF16),
        pltpu.VMEM((CTRL, HALF), BF16),
        pltpu.VMEM((2 * COLS, HALF), BF16),
        pltpu.VMEM((2, 1, COLS), F32),
        pltpu.VMEM((4, ROWS, COLS), BF16),
        pltpu.VMEM((ROWS, HALF), BF16),
        pltpu.VMEM((ROWS, 128), F32),
        pltpu.VMEM((ROWS, 128), F32),
        pltpu.VMEM((ROWS, CTRL), BF16),
        pltpu.VMEM((CHUNKS, 5 * CHUNK, 128), BF16),
        pltpu.VMEM((CHUNKS, CHUNK, CHUNK), F32),
        pltpu.VMEM((2, ROWS, 128), F32),
        pltpu.VMEM((2, ROWS, 128), F32),
        pltpu.VMEM((2, CHUNKS, 8, 128), F32),
        pltpu.VMEM((2, CHUNKS, 8, 128), F32),
        pltpu.VMEM((2, ROWS, COLS), BF16),
        pltpu.VMEM((2, ROWS, COLS), BF16),
        pltpu.VMEM((2, ROWS, COLS), F32),
        pltpu.VMEM((2, 2, ROWS, COLS), BF16),
        pltpu.VMEM((2 * CHUNKS, STATE, 2 * COLS), F32),
        pltpu.VMEM((CHUNKS + 1, 8, 128), F32),
        pltpu.VMEM((2, CHUNKS, 8, COLS), F32),
        pltpu.VMEM((NSEQ, 8, 128), F32),
        pltpu.VMEM((NSEQ, 8, 2 * COLS), F32),
        pltpu.VMEM((2, NSEQ, 2 * GROUP, COLS), BF16),
        pltpu.VMEM((2, NSEQ, 2 * GROUP, COLS), BF16),
        pltpu.VMEM((NSEQ, 2, GROUP, COLS), F32),
        pltpu.VMEM((2, NSEQ, 2 * GROUP, COLS), BF16),
        pltpu.VMEM((2, NSEQ, 2 * GROUP, COLS), BF16),
        pltpu.VMEM((2, ROWS, COLS), F32),
        pltpu.VMEM((2, ROWS, COLS), F32),
        pltpu.VMEM((2, 3, 8, HALF_ROWS), F32),
        pltpu.VMEM((2, 8, HALF_ROWS), F32),
        pltpu.VMEM((ROWS, 2 * COLS), BF16),
        pltpu.VMEM((4, ROWS, COLS), BF16),
        pltpu.VMEM((2, ROWS, COLS), BF16),
        pltpu.VMEM((2, 2, CHUNK, COLS), BF16),
        dma((5,)),
        dma((7,)),
        dma((7,)),
        dma((3, 10)),
        dma((3, 10)),
        dma((NSEQ,)),
        dma((NSEQ,)),
        dma((2, NSEQ)),
        dma((2, NSEQ)),
        dma((2, NSEQ)),
        dma((2, NSEQ)),
        dma((2, 3)),
        dma((2, 3)),
        dma((2, 6)),
        dma((2, 6)),
    ]
    return pl.pallas_call(
        kernel,
        name="mixer",
        out_shape=jax.ShapeDtypeStruct((ROWS, COLS), BF16),
        in_specs=[hbm, vmem, hbm, hbm, hbm, vmem, vmem, vmem, vmem, hbm, smem],
        out_specs=vmem,
        scratch_shapes=scratch,
        compiler_params=pltpu.CompilerParams(
            collective_id=0, has_side_effects=True, vmem_limit_bytes=56 * 2**20
        ),
    )(
        hidden,
        norm_gain.reshape(4, 1, COLS),
        w_values,
        w_gates,
        w_control.T,
        dt_bias.reshape(1, HEADS),
        decay_total.reshape(1, HEADS),
        skip_gain.reshape(1, HEADS),
        gate_gain.reshape(1, COLS),
        w_out,
        doc_starts,
    )


def solution(mesh):
    in_specs = (
        P("seq", "chan"),
        P(),
        P(None, "chan"),
        P(None, "chan"),
        P(),
        P(),
        P(),
        P(),
        P("chan"),
        P("chan", None),
        P(),
    )
    return jax.shard_map(local, mesh=mesh, in_specs=in_specs, out_specs=P("seq", "chan"), check_vma=False)
```

```python
import jax
import jax.numpy as jnp
from jax import lax
from jax.experimental import pallas as pl
from jax.experimental.pallas import tpu as pltpu
from jax.sharding import PartitionSpec as P

MESH = pl.DeviceIdType.MESH
F32 = jnp.float32
BF16 = jnp.bfloat16
HIGHEST = lax.Precision.HIGHEST

HEAD_DIM = 64
STATE = 128
CHUNK = 128
ROWS = 512
COLS = 512
HALF = 2048
HEADS = 64
NCHAN = 8
NSEQ = 16
CHUNKS = ROWS // CHUNK
PAIRS = COLS // 128
BLOCK_HEADS = COLS // HEAD_DIM
GROUP = STATE // NSEQ
HALF_ROWS = ROWS // 2
CTRL = 2 * STATE + HEADS
LOG2E = 1.4426950408889634
norm_eps = 1e-05


def dot(a, b):
    return jnp.dot(a, b, preferred_element_type=F32)


def dot_nt(a, b):
    return lax.dot_general(a, b, (((1,), (1,)), ((), ())), preferred_element_type=F32)


def dot_tn(a, b):
    return lax.dot_general(a, b, (((0,), (0,)), ((), ())), preferred_element_type=F32)


def exact(rows, table):
    return jnp.dot(rows, table, precision=HIGHEST, preferred_element_type=F32)


def iota(shape, dim):
    return lax.broadcasted_iota(jnp.int32, shape, dim)


def remote(src, dst, send_sem, recv_sem, device):
    return pltpu.make_async_remote_copy(
        src_ref=src,
        dst_ref=dst,
        send_sem=send_sem,
        recv_sem=recv_sem,
        device_id=device,
        device_id_type=MESH,
    )


def kernel(
    x_hbm, gain_ref, wv_hbm, wg_hbm, wc_hbm, bias_ref, decay_ref, skip_ref, ggain_ref, wo_hbm, docs,
    out_ref,
    x_v, wv, wg, wc, wo, gg, gath, xg, sumsq, rinv,
    c_sc, factors, scores_sc, l_sc, e_sc, lt_sc, et_sc, wval, val, act, reach, chunk_state, tot_sc, totx,
    log_recv, keep_x, st_send, st_recv, enter, en_send, en_recv, inner, y_f, y_b,
    ps_buf, ps_mine, comb, part, rs_buf, relay,
    loc_sem, word, ag_send, ag_recv, w_send, w_recv, s0_send, s0_recv, s1_send, s1_recv, s2_send, s2_recv,
    ps_send, ps_recv, rs_send, rs_recv,
):
    seq = lax.axis_index("seq")
    chan = lax.axis_index("chan")
    yy = chan // 2
    zz = chan % 2
    y_near = yy + 1 - 2 * (yy % 2)
    c_n = y_near * 2 + zz
    c_o = yy * 2 + 1 - zz
    c_d = y_near * 2 + 1 - zz
    c_w = (3 - yy) * 2 + zz
    mirrored = chan >= 4

    def block_of(c):
        return jnp.where(mirrored, 7 - c, c)

    k_me, k_n, k_o, k_d = block_of(chan), block_of(c_n), block_of(c_o), block_of(c_d)
    to_n, to_o, to_d, to_w = {"chan": c_n}, {"chan": c_o}, {"chan": c_d}, {"chan": c_w}
    to_right, to_left = {"seq": (seq + 4) % NSEQ}, {"seq": (seq + 12) % NSEQ}
    to_twin = {"seq": seq + 1 - 2 * (seq % 2)}
    q_me = (seq // 4) * 2 + seq % 2
    q_twin = (seq // 4) * 2 + 1 - seq % 2

    barrier = pltpu.get_barrier_semaphore()
    for device in (to_n, to_o, to_d, to_w):
        pl.semaphore_signal(barrier, inc=1, device_id=device, device_id_type=MESH)

    to_across = {"seq": seq + 2 - 4 * ((seq // 2) % 2)}
    near = (to_right, to_left, to_twin, to_across)
    for device in near:
        pl.semaphore_signal(barrier, inc=1, device_id=device, device_id_type=MESH)

    def spread_word(i):
        for device in near:
            pl.semaphore_signal(word.at[i], inc=1, device_id=device, device_id_type=MESH)

    def hear(i):
        pl.semaphore_wait(word.at[i], 4)

    x_copy = pltpu.make_async_copy(x_hbm, x_v, loc_sem.at[0])
    x_copy.start()
    v_copy = pltpu.make_async_copy(wv_hbm, wv.at[0], loc_sem.at[1])
    c_copy = pltpu.make_async_copy(wc_hbm, wc, loc_sem.at[2])
    g_copy = pltpu.make_async_copy(wg_hbm, wg.at[0], loc_sem.at[3])
    o_copy = pltpu.make_async_copy(wo_hbm, wo.at[pl.ds(0, COLS)], loc_sem.at[4])

    col = iota((COLS, COLS), 1)
    wanted = jnp.where(mirrored, COLS - 1 - col, col)
    flip = jnp.where(iota((COLS, COLS), 0) == wanted, 1.0, 0.0).astype(BF16)
    x_copy.wait()
    gath[k_me] = dot(x_v[...], flip).astype(BF16)
    gg[0] = ggain_ref[...]

    pl.semaphore_wait(barrier, 8)

    started = []

    def send(src, dst, send_sem, recv_sem, device):
        copy = remote(src, dst, send_sem, recv_sem, device)
        copy.start()
        started.append(copy)

    def ag(half, kind, block, q, device):
        ref = gath.at[block, pl.ds((2 * half + q) * CHUNK, CHUNK)]
        send(ref, ref, ag_send.at[half, kind], ag_recv.at[half, kind], device)

    def ag_wait(half, kind, block, q):
        ref = gath.at[block, pl.ds((2 * half + q) * CHUNK, CHUNK)]
        remote(ref, ref, ag_send.at[half, kind], ag_recv.at[half, kind], to_n).wait_recv()

    tensors = ((wv_hbm, wv, HALF // 8), (wg_hbm, wg, HALF // 8))

    def w_rows(t, dx, twin, half):
        size = tensors[t][2]
        q = ((q_twin if twin else q_me) + 2 * dx) % 8
        if half is None:
            return pl.ds(pl.multiple_of(q * size, size), size)
        return pl.ds(pl.multiple_of(q * size + half * (size // 2), size // 2), size // 2)

    def w_from_partner(t):
        hbm, buf, _ = tensors[t]
        rows = w_rows(t, 0, False, None)
        send(hbm.at[rows], buf.at[1, rows], w_send.at[t, 0], w_recv.at[t, 0], to_w)

    def w_on(t, kind, dx, half, device):
        ref = tensors[t][1].at[1, w_rows(t, dx, False, half)]
        send(ref, ref, w_send.at[t, kind], w_recv.at[t, kind], device)

    def w_wait(t, kind, dx, twin, half):
        ref = tensors[t][1].at[1, w_rows(t, dx, twin, half)]
        remote(ref, ref, w_send.at[t, kind], w_recv.at[t, kind], to_w).wait_recv()

    def w_stage1(t):
        w_wait(t, 0, 0, False, None)
        w_on(t, 1, 0, None, to_right)
        w_on(t, 2, 0, None, to_left)
        w_on(t, 3, 0, None, to_twin)

    def w_stage2(t):
        w_wait(t, 1, 3, False, None)
        w_on(t, 4, 3, 0, to_right)
        w_on(t, 5, 3, None, to_twin)
        w_wait(t, 2, 1, False, None)
        w_on(t, 6, 1, 1, to_left)
        w_on(t, 7, 1, None, to_twin)

    def w_stage3(t):
        w_wait(t, 4, 2, False, 0)
        w_on(t, 8, 2, 0, to_twin)
        w_wait(t, 6, 2, False, 1)
        w_on(t, 9, 2, 1, to_twin)

    def wo_rows(core, block):
        return pl.ds(pl.multiple_of(block * COLS + core * HALF_ROWS, HALF_ROWS), HALF_ROWS)

    core = seq % 2

    def wo_from_partner():
        send(wo_hbm.at[wo_rows(core, 0)], wo.at[wo_rows(core, 1)], w_send.at[2, 0], w_recv.at[2, 0], to_w)

    def wo_to_twin():
        ref = wo.at[wo_rows(core, 1)]
        remote(ref, ref, w_send.at[2, 0], w_recv.at[2, 0], to_w).wait_recv()
        send(ref, ref, w_send.at[2, 1], w_recv.at[2, 1], to_twin)

    def wo_finish():
        ref = wo.at[wo_rows(1 - core, 1)]
        remote(ref, ref, w_send.at[2, 1], w_recv.at[2, 1], to_w).wait_recv()

    def w_finish(t):
        w_wait(t, 3, 0, True, None)
        w_wait(t, 5, 3, True, None)
        w_wait(t, 7, 1, True, None)
        w_wait(t, 8, 2, True, 0)
        w_wait(t, 9, 2, True, 1)

    def ag_own(half):
        ag(half, 0, k_me, 0, to_n)
        ag(half, 2, k_me, 1, to_o)
        ag(half, 1, k_me, 1, to_n)
        ag(half, 3, k_me, 0, to_o)

    def ag_relay(half):
        ag_wait(half, 0, k_n, 0)
        ag(half, 4, k_n, 0, to_o)
        ag_wait(half, 2, k_o, 1)
        ag(half, 5, k_o, 1, to_n)

    def ag_near(half):
        ag_wait(half, 1, k_n, 1)
        scale_block(k_n, half)
        ag_wait(half, 3, k_o, 0)
        scale_block(k_o, half)

    def ag_far(half):
        ag_wait(half, 4, k_d, 0)
        ag_wait(half, 5, k_d, 1)
        scale_block(k_d, half)

    ag_own(0)
    w_from_partner(0)
    spread_word(0)
    w_from_partner(1)
    send(ggain_ref, gg.at[1], ag_send.at[0, 6], ag_recv.at[0, 6], to_w)
    for copy in (v_copy, c_copy, g_copy, o_copy):
        copy.start()

    def scale_block(k, half):
        gain = gain_ref[k]
        lanes = pl.ds(pl.multiple_of(k * COLS, COLS), COLS)

        def scale_rows(i, carry_):
            rows = pl.ds(pl.multiple_of(i * 64, 64), 64)
            x = gath[k, rows, :].astype(F32)
            xg[rows, lanes] = (x * gain).astype(BF16)
            sq = x * x
            sumsq[rows, :] += sq[:, 0:128] + sq[:, 128:256] + sq[:, 256:384] + sq[:, 384:512]
            return carry_

        lax.fori_loop(4 * half, 4 * half + 4, scale_rows, 0)

    sumsq[...] = jnp.zeros_like(sumsq)
    scale_block(k_me, 0)

    lane = iota((HEADS, 128), 1)
    head = iota((HEADS, 128), 0)
    picked = ((head == chan * BLOCK_HEADS + lane) & (lane < BLOCK_HEADS)) | (
        (head == (c_w - 1) * BLOCK_HEADS + lane) & (lane >= BLOCK_HEADS) & (lane < 2 * BLOCK_HEADS)
    )
    pick = jnp.where(picked, 1.0, 0.0)
    spread = jnp.where(iota((128, 2 * COLS), 0) == iota((128, 2 * COLS), 1) // HEAD_DIM, 1.0, 0.0)
    pick_b = pick.astype(BF16)
    spread_b = spread.astype(BF16)

    def head_row(ref):
        return exact(jnp.broadcast_to(ref[...], (8, HEADS)), pick)

    bias = head_row(bias_ref)[0:1]
    slope = head_row(decay_ref)[0:1] * (-LOG2E / (ROWS * NSEQ))
    skip_x = exact(head_row(skip_ref), spread)[0:1]

    starts = [docs[k] for k in range(4)]
    base = seq * ROWS

    def seg_at(position):
        total = jnp.int32(0)
        for start in starts:
            total = total + jnp.where(position >= start, 1, 0)
        return total

    def same(a, b):
        return jnp.where(seg_at(a) == seg_at(b), 1.0, 0.0)

    def keep_f(begin, end):
        return same(end, begin - 1)

    def keep_b(begin, end):
        return same(begin, end + 1)

    sub = iota((CHUNK, CHUNK), 0)
    lan = iota((CHUNK, CHUNK), 1)
    lower = jnp.where(sub >= lan, 1.0, 0.0).astype(BF16)
    upper = jnp.where(sub <= lan, 1.0, 0.0).astype(BF16)

    def row_scale(half):
        for i in range(2 * half, 2 * half + 2):
            rows = pl.ds(i * CHUNK, CHUNK)
            total = jnp.sum(sumsq[rows, :], axis=1, keepdims=True)
            rinv[rows, :] = jnp.broadcast_to(lax.rsqrt(total * (1.0 / HALF) + norm_eps), (CHUNK, 128))

    def project_control(half):
        rows = pl.ds(half * HALF_ROWS, HALF_ROWS)
        c_sc[rows, :] = (dot_nt(xg[rows, :], wc[...]) * rinv[rows, :][:, 0:1]).astype(BF16)

    def project_values(blk, half):
        rows = pl.ds(half * HALF_ROWS, HALF_ROWS)
        val[blk, rows, :] = (dot(xg[rows, :], wv[blk]) * rinv[rows, :][:, 0:1]).astype(BF16)

    def project_gates(blk):
        def go(i, carry_):
            rows = pl.ds(pl.multiple_of(i * HALF_ROWS, HALF_ROWS), HALF_ROWS)
            g = (dot(xg[rows, :], wg[blk]) * rinv[rows, :][:, 0:1]).astype(BF16).astype(F32)
            act[blk, rows, :] = g / (1.0 + jnp.exp(-g))
            return carry_

        lax.fori_loop(0, 2, go, 0)

    def compact(c, carry_):
        rows = pl.ds(pl.multiple_of(c * CHUNK, CHUNK), CHUNK)
        begin = base + c * CHUNK
        end = begin + CHUNK - 1
        ctl = c_sc[rows, :]
        z = dot(ctl[:, 2 * STATE :], pick_b) + bias
        step = jnp.maximum(z, 0.0) + jnp.log1p(jnp.exp(-jnp.abs(z)))
        log_rate = slope * step
        p1 = log_rate.astype(BF16)
        rest = log_rate - p1.astype(F32)
        p2 = rest.astype(BF16)
        p3 = (rest - p2.astype(F32)).astype(BF16)
        run = dot(lower, p1) + dot(lower, p2) + dot(lower, p3)
        before = run - log_rate
        total = run[CHUNK - 1 : CHUNK, :]
        l_sc[0, rows, :] = run
        e_sc[0, rows, :] = before
        l_sc[1, rows, :] = pltpu.roll(run, 128 - BLOCK_HEADS, 1)
        e_sc[1, rows, :] = pltpu.roll(before, 128 - BLOCK_HEADS, 1)
        run_t = run.T
        before_t = before.T
        for blk in range(2):
            lt_sc[blk, c] = run_t[blk * BLOCK_HEADS : (blk + 1) * BLOCK_HEADS, :]
            et_sc[blk, c] = before_t[blk * BLOCK_HEADS : (blk + 1) * BLOCK_HEADS, :]
        tot_sc[c] = jnp.broadcast_to(total, (8, 128))
        seg = seg_at(begin + sub)

        def mask(position):
            return jnp.where(seg == seg_at(position), 1.0, 0.0)

        out_f = jnp.exp2(total - run) * mask(end)
        out_b = jnp.exp2(before) * mask(begin)
        in_f = jnp.exp2(run) * mask(begin - 1)
        in_b = jnp.exp2(total - before) * mask(end + 1)
        factors[c] = jnp.concatenate([step, step * out_f, step * out_b, in_f, in_b], axis=0).astype(BF16)
        scores = dot_nt(ctl[:, STATE : 2 * STATE], ctl[:, 0:STATE])
        scores_sc[c] = jnp.where(seg == seg_at(begin + lan), scores, 0.0)
        return carry_

    def states_of(blk, first):
        spread_blk = spread_b[:, blk * COLS : (blk + 1) * COLS]

        def states(c, carry_):
            rows = pl.ds(pl.multiple_of(c * CHUNK, CHUNK), CHUNK)
            v = val[blk, rows, :].astype(F32)
            wide = dot(factors[c], spread_blk)
            wval[blk, rows, :] = (wide[0:CHUNK] * v).astype(BF16)
            weighted = jnp.concatenate(
                [wide[CHUNK : 2 * CHUNK] * v, wide[2 * CHUNK : 3 * CHUNK] * v], axis=1
            ).astype(BF16)
            reach[blk, 0, rows, :] = wide[3 * CHUNK : 4 * CHUNK].astype(BF16)
            reach[blk, 1, rows, :] = wide[4 * CHUNK : 5 * CHUNK].astype(BF16)
            chunk_state[blk * CHUNKS + c] = dot_tn(c_sc[rows, 0:STATE], weighted)
            return carry_

        lax.fori_loop(first, first + 2, states, 0)

    spread_of = [spread[:, 0:COLS], spread[:, COLS:]]

    def leave(blk):
        for c in range(CHUNKS):
            totx[blk, c] = jnp.exp2(exact(tot_sc[c], spread_of[blk]))
        f = chunk_state[blk * CHUNKS, :, 0:COLS]
        for c in range(1, CHUNKS):
            begin = base + c * CHUNK
            f = chunk_state[blk * CHUNKS + c, :, 0:COLS] + (
                totx[blk, c, 0:1, :] * keep_f(begin, begin + CHUNK - 1)
            ) * f
        b = chunk_state[blk * CHUNKS + CHUNKS - 1, :, COLS:]
        for c in range(CHUNKS - 2, -1, -1):
            begin = base + c * CHUNK
            b = chunk_state[blk * CHUNKS + c, :, COLS:] + (
                totx[blk, c, 0:1, :] * keep_b(begin, begin + CHUNK - 1)
            ) * b
        st_send[blk] = jnp.concatenate(
            [f.reshape(NSEQ, GROUP, COLS), b.reshape(NSEQ, GROUP, COLS)], axis=1
        ).astype(BF16)

        def send_state(k, carry_):
            state_copy(blk, k).start()
            return carry_

        lax.fori_loop(1, NSEQ, send_state, 0)
        st_recv[blk, seq] = st_send[blk, seq]

    def state_copy(blk, k):
        peer = (seq + k) % NSEQ
        return remote(
            st_send.at[blk, peer], st_recv.at[blk, seq], s1_send.at[blk, k], s1_recv.at[blk, k], {"seq": peer}
        )

    left = iota((CHUNK, 128), 1) < HEAD_DIM

    def within_of(blk, first):
        def within(c, carry_):
            rows = pl.ds(pl.multiple_of(c * CHUNK, CHUNK), CHUNK)
            scores = scores_sc[c]
            run = l_sc[blk, rows, :]
            before = e_sc[blk, rows, :]
            run_t = lt_sc[blk, c]
            before_t = et_sc[blk, c]
            for pair in range(PAIRS):
                fs, bs = [], []
                for h in (2 * pair, 2 * pair + 1):
                    gap = jnp.minimum(
                        run[:, h : h + 1] - run_t[h : h + 1, :],
                        before_t[h : h + 1, :] - before[:, h : h + 1],
                    )
                    g = (jnp.exp2(gap) * scores).astype(BF16)
                    fs.append(g * lower)
                    bs.append(g * upper)
                lhs = jnp.concatenate(
                    [jnp.concatenate(fs, axis=1), jnp.concatenate(bs, axis=1)], axis=0
                )
                lanes = slice(pair * 128, pair * 128 + 128)
                w = wval[blk, rows, lanes].astype(F32)
                rhs = jnp.concatenate([jnp.where(left, w, 0.0), jnp.where(left, 0.0, w)], axis=0)
                y = dot(lhs, rhs.astype(BF16))
                wide = slice(blk * COLS + pair * 128, blk * COLS + pair * 128 + 128)
                direct = skip_x[:, wide] * val[blk, rows, lanes].astype(F32)
                y_f[blk, rows, lanes] = y[0:CHUNK] + direct
                y_b[blk, rows, lanes] = y[CHUNK:] + direct
            return carry_

        lax.fori_loop(first, first + 2, within, 0)

    ag_relay(0)
    ag_own(1)
    hear(0)
    spread_word(1)
    scale_block(k_me, 1)
    ag_near(0)
    w_stage1(0)
    hear(1)
    spread_word(2)
    ag_far(0)
    row_scale(0)
    c_copy.wait()
    project_control(0)
    v_copy.wait()
    project_values(0, 0)
    ag_relay(1)
    lax.fori_loop(0, 2, compact, 0)
    w_stage2(0)
    w_stage1(1)
    wo_from_partner()
    states_of(0, 0)
    within_of(0, 0)
    w_stage3(0)

    ag_near(1)
    ag_far(1)
    row_scale(1)
    project_control(1)
    project_values(0, 1)
    lax.fori_loop(2, 4, compact, 0)
    hear(2)
    tot_sc[CHUNKS] = tot_sc[0] + tot_sc[1] + tot_sc[2] + tot_sc[3]
    log_recv[seq] = tot_sc[CHUNKS]

    def log_copy(k):
        peer = (seq + k) % NSEQ
        return remote(
            tot_sc.at[CHUNKS], log_recv.at[seq], s0_send.at[k], s0_recv.at[k], {"seq": peer}
        )

    def send_log(k, carry_):
        log_copy(k).start()
        return carry_

    lax.fori_loop(1, NSEQ, send_log, 0)

    states_of(0, 2)
    w_stage2(1)
    leave(0)
    w_finish(0)
    project_values(1, 0)
    project_values(1, 1)
    states_of(1, 0)
    w_stage3(1)
    states_of(1, 2)
    leave(1)

    def await_log(k, carry_):
        src = (seq + NSEQ - k) % NSEQ
        remote(
            tot_sc.at[CHUNKS], log_recv.at[src], s0_send.at[k], s0_recv.at[k], {"seq": src}
        ).wait_recv()
        return carry_

    def scan_devices(blk):
        def await_state(k, carry_):
            src = (seq + NSEQ - k) % NSEQ
            remote(
                st_send.at[blk, src], st_recv.at[blk, src], s1_send.at[blk, k], s1_recv.at[blk, k], {"seq": src}
            ).wait_recv()
            return carry_

        lax.fori_loop(1, NSEQ, await_state, 0)
        lanes = slice(blk * COLS, (blk + 1) * COLS)
        now = jnp.zeros((GROUP, COLS), F32)
        for d in range(NSEQ):
            enter[d, blk] = now
            if d < NSEQ - 1:
                begin = d * ROWS
                kept = keep_x[d, :, lanes] * keep_f(begin, begin + ROWS - 1)
                now = st_recv[blk, d].astype(F32)[0:GROUP] + kept * now
        now = jnp.zeros((GROUP, COLS), F32)
        for d in range(NSEQ - 1, -1, -1):
            en_send[blk, d] = jnp.concatenate([enter[d, blk], now], axis=0).astype(BF16)
            if d > 0:
                begin = d * ROWS
                kept = keep_x[d, :, lanes] * keep_b(begin, begin + ROWS - 1)
                now = st_recv[blk, d].astype(F32)[GROUP : 2 * GROUP] + kept * now

        def send_enter(k, carry_):
            enter_copy(blk, k).start()
            return carry_

        lax.fori_loop(1, NSEQ, send_enter, 0)
        en_recv[blk, seq] = en_send[blk, seq]

    def enter_copy(blk, k):
        peer = (seq + k) % NSEQ
        return remote(
            en_send.at[blk, peer], en_recv.at[blk, seq], s2_send.at[blk, k], s2_recv.at[blk, k], {"seq": peer}
        )

    lax.fori_loop(1, NSEQ, await_log, 0)
    keep_x[...] = jnp.exp2(exact(log_recv[...].reshape(NSEQ * 8, 128), spread)).reshape(NSEQ, 8, 2 * COLS)
    scan_devices(0)
    within_of(0, 2)
    g_copy.wait()
    project_gates(0)
    scan_devices(1)
    wo_to_twin()
    within_of(1, 0)
    within_of(1, 2)
    w_finish(1)
    project_gates(1)

    def outside(blk):
        def await_enter(k, carry_):
            src = (seq + NSEQ - k) % NSEQ
            remote(
                en_send.at[blk, src], en_recv.at[blk, src], s2_send.at[blk, k], s2_recv.at[blk, k], {"seq": src}
            ).wait_recv()
            return carry_

        lax.fori_loop(1, NSEQ, await_enter, 0)
        both = en_recv[blk].astype(F32)
        f = both[:, 0:GROUP].reshape(STATE, COLS)
        b = both[:, GROUP : 2 * GROUP].reshape(STATE, COLS)
        for c in range(CHUNKS):
            begin = base + c * CHUNK
            inner[blk, c, 0] = f.astype(BF16)
            if c < CHUNKS - 1:
                f = chunk_state[blk * CHUNKS + c, :, 0:COLS] + (
                    totx[blk, c, 0:1, :] * keep_f(begin, begin + CHUNK - 1)
                ) * f
        for c in range(CHUNKS - 1, -1, -1):
            begin = base + c * CHUNK
            inner[blk, c, 1] = b.astype(BF16)
            if c > 0:
                b = chunk_state[blk * CHUNKS + c, :, COLS:] + (
                    totx[blk, c, 0:1, :] * keep_b(begin, begin + CHUNK - 1)
                ) * b

    outside(0)
    outside(1)

    ones = jnp.ones((8, COLS), BF16)
    row8 = iota((8, CHUNK), 0)

    def gate(c, carry_):
        rows = pl.ds(pl.multiple_of(c * CHUNK, CHUNK), CHUNK)
        sums = jnp.zeros((8, CHUNK), F32)
        cc = c_sc[rows, STATE : 2 * STATE]
        for blk in range(2):
            a = act[blk, rows, :]
            for d, y in enumerate((y_f, y_b)):
                added = dot(cc, inner[blk, c, d]) * reach[blk, d, rows, :].astype(F32)
                v = (y[blk, rows, :] + added) * a
                y[blk, rows, :] = v
                sq = v * v
                hi = sq.astype(BF16)
                lo = (sq - hi.astype(F32)).astype(BF16)
                sums = sums + jnp.where(row8 == d, dot_nt(ones, hi) + dot_nt(ones, lo), 0.0)
        ps_mine[c // 2, :, pl.ds(pl.multiple_of((c % 2) * CHUNK, CHUNK), CHUNK)] = sums
        return carry_

    def send_sums(half):
        for k, device in enumerate((to_d, to_n, to_o)):
            send(ps_mine.at[half], ps_buf.at[half, k], ps_send.at[half, k], ps_recv.at[half, k], device)

    def norm_half(half):
        for k in range(3):
            remote(
                ps_mine.at[half], ps_buf.at[half, k], ps_send.at[half, k], ps_recv.at[half, k], to_n
            ).wait_recv()
        sums = ps_mine[half] + ps_buf[half, 0] + ps_buf[half, 1] + ps_buf[half, 2]
        scale = lax.rsqrt(sums * (1.0 / (COLS * NCHAN)) + norm_eps)
        scale = jnp.concatenate([scale, jnp.zeros((CHUNK - 8, HALF_ROWS), F32)], axis=0)
        for i in range(2):
            c = 2 * half + i
            rows = slice(c * CHUNK, (c + 1) * CHUNK)
            r = scale[:, i * CHUNK : (i + 1) * CHUNK].T
            for blk in range(2):
                both = y_f[blk, rows, :] * r[:, 0:1] + y_b[blk, rows, :] * r[:, 1:2]
                comb[rows, blk * COLS : (blk + 1) * COLS] = (both * gg[blk]).astype(BF16)

    lax.fori_loop(0, 2, gate, 0)
    send_sums(0)
    lax.fori_loop(2, 4, gate, 0)
    send_sums(1)
    wo_finish()
    o_copy.wait()
    remote(ggain_ref, gg.at[1], ag_send.at[0, 6], ag_recv.at[0, 6], to_w).wait_recv()

    def out_block(k, half):
        lanes = pl.ds(pl.multiple_of(k * COLS, COLS), COLS)
        rows = pl.ds(half * HALF_ROWS, HALF_ROWS)
        part[k, rows, :] = dot(comb[rows, :], wo[:, lanes]).astype(BF16)

    def quarter(half, i):
        return pl.ds((2 * half + i) * CHUNK, CHUNK)

    def rs(half, kind, src, dst, device):
        send(src, dst, rs_send.at[half, kind], rs_recv.at[half, kind], device)

    def rs_wait(half, kind, dst):
        remote(
            part.at[k_me, quarter(0, 0)], dst, rs_send.at[half, kind], rs_recv.at[half, kind], to_n
        ).wait_recv()

    def add(block, rows, ref):
        part[block, rows, :] = (part[block, rows, :].astype(F32) + ref[...].astype(F32)).astype(BF16)

    def produce(half):
        q1, q2 = quarter(half, 0), quarter(half, 1)
        out_block(k_d, half)
        rs(half, 0, part.at[k_d, q1], relay.at[half, 0], to_o)
        rs(half, 1, part.at[k_d, q2], relay.at[half, 1], to_n)
        out_block(k_n, half)
        rs(half, 2, part.at[k_n, q2], rs_buf.at[0, q2], to_n)
        out_block(k_o, half)
        rs(half, 4, part.at[k_o, q1], rs_buf.at[1, q1], to_o)

    def hand_on(half):
        q1, q2 = quarter(half, 0), quarter(half, 1)
        rs_wait(half, 0, relay.at[half, 0])
        add(k_n, q1, relay.at[half, 0])
        rs(half, 3, part.at[k_n, q1], rs_buf.at[0, q1], to_n)
        rs_wait(half, 1, relay.at[half, 1])
        add(k_o, q2, relay.at[half, 1])
        rs(half, 5, part.at[k_o, q2], rs_buf.at[1, q2], to_o)

    def finish(half):
        q1, q2 = quarter(half, 0), quarter(half, 1)
        rs_wait(half, 4, rs_buf.at[1, q1])
        rs_wait(half, 2, rs_buf.at[0, q2])
        rs_wait(half, 3, rs_buf.at[0, q1])
        rs_wait(half, 5, rs_buf.at[1, q2])
        rows = pl.ds(half * HALF_ROWS, HALF_ROWS)
        total = part[k_me, rows, :].astype(F32) + rs_buf[0, rows, :].astype(F32) + rs_buf[1, rows, :].astype(F32)
        out_ref[rows, :] = dot(total.astype(BF16), flip).astype(BF16)

    norm_half(0)
    produce(0)
    norm_half(1)
    hand_on(0)
    produce(1)
    out_block(k_me, 0)
    out_block(k_me, 1)
    hand_on(1)
    finish(0)
    finish(1)

    for copy in started:
        copy.wait_send()

    def sent_seq(k, carry_):
        log_copy(k).wait_send()
        for blk in range(2):
            state_copy(blk, k).wait_send()
            enter_copy(blk, k).wait_send()
        return carry_

    lax.fori_loop(1, NSEQ, sent_seq, 0)


def local(
    hidden, norm_gain, w_values, w_gates, w_control, dt_bias, decay_total, skip_gain, gate_gain, w_out, doc_starts
):
    vmem = pl.BlockSpec(memory_space=pltpu.VMEM)
    hbm = pl.BlockSpec(memory_space=pl.ANY)
    smem = pl.BlockSpec(memory_space=pltpu.SMEM)
    dma = pltpu.SemaphoreType.DMA
    scratch = [
        pltpu.VMEM((ROWS, COLS), BF16),
        pltpu.VMEM((2, HALF, COLS), BF16),
        pltpu.VMEM((2, HALF, COLS), BF16),
        pltpu.VMEM((CTRL, HALF), BF16),
        pltpu.VMEM((2 * COLS, HALF), BF16),
        pltpu.VMEM((2, 1, COLS), F32),
        pltpu.VMEM((4, ROWS, COLS), BF16),
        pltpu.VMEM((ROWS, HALF), BF16),
        pltpu.VMEM((ROWS, 128), F32),
        pltpu.VMEM((ROWS, 128), F32),
        pltpu.VMEM((ROWS, CTRL), BF16),
        pltpu.VMEM((CHUNKS, 5 * CHUNK, 128), BF16),
        pltpu.VMEM((CHUNKS, CHUNK, CHUNK), F32),
        pltpu.VMEM((2, ROWS, 128), F32),
        pltpu.VMEM((2, ROWS, 128), F32),
        pltpu.VMEM((2, CHUNKS, 8, 128), F32),
        pltpu.VMEM((2, CHUNKS, 8, 128), F32),
        pltpu.VMEM((2, ROWS, COLS), BF16),
        pltpu.VMEM((2, ROWS, COLS), BF16),
        pltpu.VMEM((2, ROWS, COLS), F32),
        pltpu.VMEM((2, 2, ROWS, COLS), BF16),
        pltpu.VMEM((2 * CHUNKS, STATE, 2 * COLS), F32),
        pltpu.VMEM((CHUNKS + 1, 8, 128), F32),
        pltpu.VMEM((2, CHUNKS, 8, COLS), F32),
        pltpu.VMEM((NSEQ, 8, 128), F32),
        pltpu.VMEM((NSEQ, 8, 2 * COLS), F32),
        pltpu.VMEM((2, NSEQ, 2 * GROUP, COLS), BF16),
        pltpu.VMEM((2, NSEQ, 2 * GROUP, COLS), BF16),
        pltpu.VMEM((NSEQ, 2, GROUP, COLS), F32),
        pltpu.VMEM((2, NSEQ, 2 * GROUP, COLS), BF16),
        pltpu.VMEM((2, NSEQ, 2 * GROUP, COLS), BF16),
        pltpu.VMEM((2, CHUNKS, 2, STATE, COLS), BF16),
        pltpu.VMEM((2, ROWS, COLS), F32),
        pltpu.VMEM((2, ROWS, COLS), F32),
        pltpu.VMEM((2, 3, 8, HALF_ROWS), F32),
        pltpu.VMEM((2, 8, HALF_ROWS), F32),
        pltpu.VMEM((ROWS, 2 * COLS), BF16),
        pltpu.VMEM((4, ROWS, COLS), BF16),
        pltpu.VMEM((2, ROWS, COLS), BF16),
        pltpu.VMEM((2, 2, CHUNK, COLS), BF16),
        dma((5,)),
        pltpu.SemaphoreType.REGULAR((3,)),
        dma((2, 7)),
        dma((2, 7)),
        dma((3, 10)),
        dma((3, 10)),
        dma((NSEQ,)),
        dma((NSEQ,)),
        dma((2, NSEQ)),
        dma((2, NSEQ)),
        dma((2, NSEQ)),
        dma((2, NSEQ)),
        dma((2, 3)),
        dma((2, 3)),
        dma((2, 6)),
        dma((2, 6)),
    ]
    return pl.pallas_call(
        kernel,
        name="mixer",
        out_shape=jax.ShapeDtypeStruct((ROWS, COLS), BF16),
        in_specs=[hbm, vmem, hbm, hbm, hbm, vmem, vmem, vmem, vmem, hbm, smem],
        out_specs=vmem,
        scratch_shapes=scratch,
        compiler_params=pltpu.CompilerParams(
            collective_id=0, has_side_effects=True, vmem_limit_bytes=56 * 2**20
        ),
    )(
        hidden,
        norm_gain.reshape(4, 1, COLS),
        w_values,
        w_gates,
        w_control.T,
        dt_bias.reshape(1, HEADS),
        decay_total.reshape(1, HEADS),
        skip_gain.reshape(1, HEADS),
        gate_gain.reshape(1, COLS),
        w_out,
        doc_starts,
    )


def solution(mesh):
    in_specs = (
        P("seq", "chan"),
        P(),
        P(None, "chan"),
        P(None, "chan"),
        P(),
        P(),
        P(),
        P(),
        P("chan"),
        P("chan", None),
        P(),
    )
    return jax.shard_map(local, mesh=mesh, in_specs=in_specs, out_specs=P("seq", "chan"), check_vma=False)
```

```python
import jax
import jax.numpy as jnp
from jax import lax
from jax.experimental import pallas as pl
from jax.experimental.pallas import tpu as pltpu
from jax.sharding import PartitionSpec as P

MESH = pl.DeviceIdType.MESH
F32 = jnp.float32
BF16 = jnp.bfloat16
HIGHEST = lax.Precision.HIGHEST

HEAD_DIM = 64
STATE = 128
CHUNK = 128
ROWS = 512
COLS = 512
HALF = 2048
HEADS = 64
NCHAN = 8
NSEQ = 16
CHUNKS = ROWS // CHUNK
PAIRS = COLS // 128
BLOCK_HEADS = COLS // HEAD_DIM
GROUP = STATE // NSEQ
HALF_ROWS = ROWS // 2
CTRL = 2 * STATE + HEADS
LOG2E = 1.4426950408889634
norm_eps = 1e-05


def dot(a, b):
    return jnp.dot(a, b, preferred_element_type=F32)


def dot_nt(a, b):
    return lax.dot_general(a, b, (((1,), (1,)), ((), ())), preferred_element_type=F32)


def dot_tn(a, b):
    return lax.dot_general(a, b, (((0,), (0,)), ((), ())), preferred_element_type=F32)


def exact(rows, table):
    return jnp.dot(rows, table, precision=HIGHEST, preferred_element_type=F32)


def iota(shape, dim):
    return lax.broadcasted_iota(jnp.int32, shape, dim)


def remote(src, dst, send_sem, recv_sem, device):
    return pltpu.make_async_remote_copy(
        src_ref=src,
        dst_ref=dst,
        send_sem=send_sem,
        recv_sem=recv_sem,
        device_id=device,
        device_id_type=MESH,
    )


def kernel(
    x_hbm, gain_ref, wv_hbm, wg_hbm, wc_hbm, bias_ref, decay_ref, skip_ref, ggain_ref, wo_hbm, docs,
    out_ref,
    x_v, wv, wg, wc, wo, gg, gath, xg, sumsq, rinv,
    c_sc, factors, scores_sc, l_sc, e_sc, lt_sc, et_sc, wval, val, act, reach, chunk_state, tot_sc, totx,
    log_recv, keep_x, st_send, st_recv, enter, en_send, en_recv, inner, y_f, y_b,
    ps_buf, ps_mine, comb, part, rs_buf, relay,
    loc_sem, word, ag_send, ag_recv, w_send, w_recv, s0_send, s0_recv, s1_send, s1_recv, s2_send, s2_recv,
    ps_send, ps_recv, rs_send, rs_recv,
):
    seq = lax.axis_index("seq")
    chan = lax.axis_index("chan")
    yy = chan // 2
    zz = chan % 2
    y_near = yy + 1 - 2 * (yy % 2)
    c_n = y_near * 2 + zz
    c_o = yy * 2 + 1 - zz
    c_d = y_near * 2 + 1 - zz
    c_w = (3 - yy) * 2 + zz
    mirrored = chan >= 4

    def block_of(c):
        return jnp.where(mirrored, 7 - c, c)

    k_me, k_n, k_o, k_d = block_of(chan), block_of(c_n), block_of(c_o), block_of(c_d)
    to_n, to_o, to_d, to_w = {"chan": c_n}, {"chan": c_o}, {"chan": c_d}, {"chan": c_w}
    to_right, to_left = {"seq": (seq + 4) % NSEQ}, {"seq": (seq + 12) % NSEQ}
    to_twin = {"seq": seq + 1 - 2 * (seq % 2)}
    q_me = (seq // 4) * 2 + seq % 2
    q_twin = (seq // 4) * 2 + 1 - seq % 2

    barrier = pltpu.get_barrier_semaphore()
    for device in (to_n, to_o, to_d, to_w):
        pl.semaphore_signal(barrier, inc=1, device_id=device, device_id_type=MESH)

    to_across = {"seq": seq + 2 - 4 * ((seq // 2) % 2)}
    near = (to_right, to_left, to_twin, to_across)
    for device in near:
        pl.semaphore_signal(barrier, inc=1, device_id=device, device_id_type=MESH)

    def spread_word(i):
        for device in near:
            pl.semaphore_signal(word.at[i], inc=1, device_id=device, device_id_type=MESH)

    def hear(i):
        pl.semaphore_wait(word.at[i], 4)

    x_copy = pltpu.make_async_copy(x_hbm, x_v, loc_sem.at[0])
    x_copy.start()
    v_copy = pltpu.make_async_copy(wv_hbm, wv.at[0], loc_sem.at[1])
    c_copy = pltpu.make_async_copy(wc_hbm, wc, loc_sem.at[2])
    g_copy = pltpu.make_async_copy(wg_hbm, wg.at[0], loc_sem.at[3])
    o_copy = pltpu.make_async_copy(wo_hbm, wo.at[pl.ds(0, COLS)], loc_sem.at[4])

    col = iota((COLS, COLS), 1)
    wanted = jnp.where(mirrored, COLS - 1 - col, col)
    flip = jnp.where(iota((COLS, COLS), 0) == wanted, 1.0, 0.0).astype(BF16)
    x_copy.wait()
    gath[k_me] = dot(x_v[...], flip).astype(BF16)
    gg[0] = ggain_ref[...]

    pl.semaphore_wait(barrier, 8)

    started = []

    def send(src, dst, send_sem, recv_sem, device):
        copy = remote(src, dst, send_sem, recv_sem, device)
        copy.start()
        started.append(copy)

    def ag(half, kind, block, q, device):
        ref = gath.at[block, pl.ds((2 * half + q) * CHUNK, CHUNK)]
        send(ref, ref, ag_send.at[half, kind], ag_recv.at[half, kind], device)

    def ag_wait(half, kind, block, q):
        ref = gath.at[block, pl.ds((2 * half + q) * CHUNK, CHUNK)]
        remote(ref, ref, ag_send.at[half, kind], ag_recv.at[half, kind], to_n).wait_recv()

    tensors = ((wv_hbm, wv, HALF // 8), (wg_hbm, wg, HALF // 8))

    def w_rows(t, dx, twin, half):
        size = tensors[t][2]
        q = ((q_twin if twin else q_me) + 2 * dx) % 8
        if half is None:
            return pl.ds(pl.multiple_of(q * size, size), size)
        return pl.ds(pl.multiple_of(q * size + half * (size // 2), size // 2), size // 2)

    def w_from_partner(t):
        hbm, buf, _ = tensors[t]
        rows = w_rows(t, 0, False, None)
        send(hbm.at[rows], buf.at[1, rows], w_send.at[t, 0], w_recv.at[t, 0], to_w)

    def w_on(t, kind, dx, half, device):
        ref = tensors[t][1].at[1, w_rows(t, dx, False, half)]
        send(ref, ref, w_send.at[t, kind], w_recv.at[t, kind], device)

    def w_wait(t, kind, dx, twin, half):
        ref = tensors[t][1].at[1, w_rows(t, dx, twin, half)]
        remote(ref, ref, w_send.at[t, kind], w_recv.at[t, kind], to_w).wait_recv()

    def w_stage1(t):
        w_wait(t, 0, 0, False, None)
        w_on(t, 1, 0, None, to_right)
        w_on(t, 2, 0, None, to_left)
        w_on(t, 3, 0, None, to_twin)

    def w_stage2(t):
        w_wait(t, 1, 3, False, None)
        w_on(t, 4, 3, 0, to_right)
        w_on(t, 5, 3, None, to_twin)
        w_wait(t, 2, 1, False, None)
        w_on(t, 6, 1, 1, to_left)
        w_on(t, 7, 1, None, to_twin)

    def w_stage3(t):
        w_wait(t, 4, 2, False, 0)
        w_on(t, 8, 2, 0, to_twin)
        w_wait(t, 6, 2, False, 1)
        w_on(t, 9, 2, 1, to_twin)

    def wo_rows(core, block):
        return pl.ds(pl.multiple_of(block * COLS + core * HALF_ROWS, HALF_ROWS), HALF_ROWS)

    core = seq % 2

    def wo_from_partner():
        send(wo_hbm.at[wo_rows(core, 0)], wo.at[wo_rows(core, 1)], w_send.at[2, 0], w_recv.at[2, 0], to_w)

    def wo_to_twin():
        ref = wo.at[wo_rows(core, 1)]
        remote(ref, ref, w_send.at[2, 0], w_recv.at[2, 0], to_w).wait_recv()
        send(ref, ref, w_send.at[2, 1], w_recv.at[2, 1], to_twin)

    def wo_finish():
        ref = wo.at[wo_rows(1 - core, 1)]
        remote(ref, ref, w_send.at[2, 1], w_recv.at[2, 1], to_w).wait_recv()

    def w_finish(t):
        w_wait(t, 3, 0, True, None)
        w_wait(t, 5, 3, True, None)
        w_wait(t, 7, 1, True, None)
        w_wait(t, 8, 2, True, 0)
        w_wait(t, 9, 2, True, 1)

    def ag_own(half):
        ag(half, 0, k_me, 0, to_n)
        ag(half, 2, k_me, 1, to_o)
        ag(half, 1, k_me, 1, to_n)
        ag(half, 3, k_me, 0, to_o)

    def ag_relay(half):
        ag_wait(half, 0, k_n, 0)
        ag(half, 4, k_n, 0, to_o)
        ag_wait(half, 2, k_o, 1)
        ag(half, 5, k_o, 1, to_n)

    def ag_near(half):
        ag_wait(half, 1, k_n, 1)
        scale_block(k_n, half)
        ag_wait(half, 3, k_o, 0)
        scale_block(k_o, half)

    def ag_far(half):
        ag_wait(half, 4, k_d, 0)
        ag_wait(half, 5, k_d, 1)
        scale_block(k_d, half)

    ag_own(0)
    w_from_partner(0)
    spread_word(0)
    w_from_partner(1)
    send(ggain_ref, gg.at[1], ag_send.at[0, 6], ag_recv.at[0, 6], to_w)
    for copy in (v_copy, c_copy, g_copy, o_copy):
        copy.start()

    def scale_block(k, half):
        gain = gain_ref[k]
        lanes = pl.ds(pl.multiple_of(k * COLS, COLS), COLS)

        def scale_rows(i, carry_):
            rows = pl.ds(pl.multiple_of(i * 64, 64), 64)
            x = gath[k, rows, :].astype(F32)
            xg[rows, lanes] = (x * gain).astype(BF16)
            sq = x * x
            sumsq[rows, :] += sq[:, 0:128] + sq[:, 128:256] + sq[:, 256:384] + sq[:, 384:512]
            return carry_

        lax.fori_loop(4 * half, 4 * half + 4, scale_rows, 0)

    sumsq[...] = jnp.zeros_like(sumsq)
    scale_block(k_me, 0)

    lane = iota((HEADS, 128), 1)
    head = iota((HEADS, 128), 0)
    picked = ((head == chan * BLOCK_HEADS + lane) & (lane < BLOCK_HEADS)) | (
        (head == (c_w - 1) * BLOCK_HEADS + lane) & (lane >= BLOCK_HEADS) & (lane < 2 * BLOCK_HEADS)
    )
    pick = jnp.where(picked, 1.0, 0.0)
    spread = jnp.where(iota((128, 2 * COLS), 0) == iota((128, 2 * COLS), 1) // HEAD_DIM, 1.0, 0.0)
    pick_b = pick.astype(BF16)
    spread_b = spread.astype(BF16)

    def head_row(ref):
        return exact(jnp.broadcast_to(ref[...], (8, HEADS)), pick)

    bias = head_row(bias_ref)[0:1]
    slope = head_row(decay_ref)[0:1] * (-LOG2E / (ROWS * NSEQ))
    skip_x = exact(head_row(skip_ref), spread)[0:1]

    starts = [docs[k] for k in range(4)]
    base = seq * ROWS

    def seg_at(position):
        total = jnp.int32(0)
        for start in starts:
            total = total + jnp.where(position >= start, 1, 0)
        return total

    def same(a, b):
        return jnp.where(seg_at(a) == seg_at(b), 1.0, 0.0)

    def keep_f(begin, end):
        return same(end, begin - 1)

    def keep_b(begin, end):
        return same(begin, end + 1)

    sub = iota((CHUNK, CHUNK), 0)
    lan = iota((CHUNK, CHUNK), 1)
    lower = jnp.where(sub >= lan, 1.0, 0.0).astype(BF16)
    upper = jnp.where(sub <= lan, 1.0, 0.0).astype(BF16)

    def row_scale(half):
        for i in range(2 * half, 2 * half + 2):
            rows = pl.ds(i * CHUNK, CHUNK)
            total = jnp.sum(sumsq[rows, :], axis=1, keepdims=True)
            rinv[rows, :] = jnp.broadcast_to(lax.rsqrt(total * (1.0 / HALF) + norm_eps), (CHUNK, 128))

    def project_control(half):
        rows = pl.ds(half * HALF_ROWS, HALF_ROWS)
        c_sc[rows, :] = (dot_nt(xg[rows, :], wc[...]) * rinv[rows, :][:, 0:1]).astype(BF16)

    def project_values(blk, half):
        rows = pl.ds(half * HALF_ROWS, HALF_ROWS)
        val[blk, rows, :] = (dot(xg[rows, :], wv[blk]) * rinv[rows, :][:, 0:1]).astype(BF16)

    def project_gates(blk):
        def go(i, carry_):
            rows = pl.ds(pl.multiple_of(i * HALF_ROWS, HALF_ROWS), HALF_ROWS)
            g = (dot(xg[rows, :], wg[blk]) * rinv[rows, :][:, 0:1]).astype(BF16).astype(F32)
            act[blk, rows, :] = g / (1.0 + jnp.exp(-g))
            return carry_

        lax.fori_loop(0, 2, go, 0)

    def compact(c, carry_):
        rows = pl.ds(pl.multiple_of(c * CHUNK, CHUNK), CHUNK)
        begin = base + c * CHUNK
        end = begin + CHUNK - 1
        ctl = c_sc[rows, :]
        z = dot(ctl[:, 2 * STATE :], pick_b) + bias
        step = jnp.maximum(z, 0.0) + jnp.log1p(jnp.exp(-jnp.abs(z)))
        log_rate = slope * step
        p1 = log_rate.astype(BF16)
        rest = log_rate - p1.astype(F32)
        p2 = rest.astype(BF16)
        p3 = (rest - p2.astype(F32)).astype(BF16)
        run = dot(lower, p1) + dot(lower, p2) + dot(lower, p3)
        before = run - log_rate
        total = run[CHUNK - 1 : CHUNK, :]
        l_sc[0, rows, :] = run
        e_sc[0, rows, :] = before
        l_sc[1, rows, :] = pltpu.roll(run, 128 - BLOCK_HEADS, 1)
        e_sc[1, rows, :] = pltpu.roll(before, 128 - BLOCK_HEADS, 1)
        run_t = run.T
        before_t = before.T
        for blk in range(2):
            lt_sc[blk, c] = run_t[blk * BLOCK_HEADS : (blk + 1) * BLOCK_HEADS, :]
            et_sc[blk, c] = before_t[blk * BLOCK_HEADS : (blk + 1) * BLOCK_HEADS, :]
        tot_sc[c] = jnp.broadcast_to(total, (8, 128))
        seg = seg_at(begin + sub)

        def mask(position):
            return jnp.where(seg == seg_at(position), 1.0, 0.0)

        out_f = jnp.exp2(total - run) * mask(end)
        out_b = jnp.exp2(before) * mask(begin)
        in_f = jnp.exp2(run) * mask(begin - 1)
        in_b = jnp.exp2(total - before) * mask(end + 1)
        factors[c] = jnp.concatenate([step, step * out_f, step * out_b, in_f, in_b], axis=0).astype(BF16)
        scores = dot_nt(ctl[:, STATE : 2 * STATE], ctl[:, 0:STATE])
        scores_sc[c] = jnp.where(seg == seg_at(begin + lan), scores, 0.0)
        return carry_

    def states_of(blk, first):
        spread_blk = spread_b[:, blk * COLS : (blk + 1) * COLS]

        def states(c, carry_):
            rows = pl.ds(pl.multiple_of(c * CHUNK, CHUNK), CHUNK)
            v = val[blk, rows, :].astype(F32)
            wide = dot(factors[c], spread_blk)
            wval[blk, rows, :] = (wide[0:CHUNK] * v).astype(BF16)
            weighted = jnp.concatenate(
                [wide[CHUNK : 2 * CHUNK] * v, wide[2 * CHUNK : 3 * CHUNK] * v], axis=1
            ).astype(BF16)
            reach[blk, 0, rows, :] = wide[3 * CHUNK : 4 * CHUNK].astype(BF16)
            reach[blk, 1, rows, :] = wide[4 * CHUNK : 5 * CHUNK].astype(BF16)
            chunk_state[blk * CHUNKS + c] = dot_tn(c_sc[rows, 0:STATE], weighted)
            return carry_

        lax.fori_loop(first, first + 2, states, 0)

    spread_of = [spread[:, 0:COLS], spread[:, COLS:]]

    def leave(blk):
        for c in range(CHUNKS):
            totx[blk, c] = jnp.exp2(exact(tot_sc[c], spread_of[blk]))
        f = chunk_state[blk * CHUNKS, :, 0:COLS]
        for c in range(1, CHUNKS):
            begin = base + c * CHUNK
            f = chunk_state[blk * CHUNKS + c, :, 0:COLS] + (
                totx[blk, c, 0:1, :] * keep_f(begin, begin + CHUNK - 1)
            ) * f
        b = chunk_state[blk * CHUNKS + CHUNKS - 1, :, COLS:]
        for c in range(CHUNKS - 2, -1, -1):
            begin = base + c * CHUNK
            b = chunk_state[blk * CHUNKS + c, :, COLS:] + (
                totx[blk, c, 0:1, :] * keep_b(begin, begin + CHUNK - 1)
            ) * b
        st_send[blk] = jnp.concatenate(
            [f.reshape(NSEQ, GROUP, COLS), b.reshape(NSEQ, GROUP, COLS)], axis=1
        ).astype(BF16)

        def send_state(k, carry_):
            state_copy(blk, k).start()
            return carry_

        lax.fori_loop(1, NSEQ, send_state, 0)
        st_recv[blk, seq] = st_send[blk, seq]

    def state_copy(blk, k):
        peer = (seq + k) % NSEQ
        return remote(
            st_send.at[blk, peer], st_recv.at[blk, seq], s1_send.at[blk, k], s1_recv.at[blk, k], {"seq": peer}
        )

    left = iota((CHUNK, 128), 1) < HEAD_DIM

    def within_of(blk, first):
        def within(c, carry_):
            rows = pl.ds(pl.multiple_of(c * CHUNK, CHUNK), CHUNK)
            scores = scores_sc[c]
            run = l_sc[blk, rows, :]
            before = e_sc[blk, rows, :]
            run_t = lt_sc[blk, c]
            before_t = et_sc[blk, c]
            for pair in range(PAIRS):
                fs, bs = [], []
                for h in (2 * pair, 2 * pair + 1):
                    gap = jnp.minimum(
                        run[:, h : h + 1] - run_t[h : h + 1, :],
                        before_t[h : h + 1, :] - before[:, h : h + 1],
                    )
                    g = (jnp.exp2(gap) * scores).astype(BF16)
                    fs.append(g * lower)
                    bs.append(g * upper)
                lhs = jnp.concatenate(
                    [jnp.concatenate(fs, axis=1), jnp.concatenate(bs, axis=1)], axis=0
                )
                lanes = slice(pair * 128, pair * 128 + 128)
                w = wval[blk, rows, lanes].astype(F32)
                rhs = jnp.concatenate([jnp.where(left, w, 0.0), jnp.where(left, 0.0, w)], axis=0)
                y = dot(lhs, rhs.astype(BF16))
                wide = slice(blk * COLS + pair * 128, blk * COLS + pair * 128 + 128)
                direct = skip_x[:, wide] * val[blk, rows, lanes].astype(F32)
                y_f[blk, rows, lanes] = y[0:CHUNK] + direct
                y_b[blk, rows, lanes] = y[CHUNK:] + direct
            return carry_

        lax.fori_loop(first, first + 2, within, 0)

    ag_relay(0)
    ag_own(1)
    hear(0)
    spread_word(1)
    scale_block(k_me, 1)
    ag_near(0)
    w_stage1(0)
    hear(1)
    spread_word(2)
    ag_far(0)
    row_scale(0)
    c_copy.wait()
    project_control(0)
    v_copy.wait()
    project_values(0, 0)
    ag_relay(1)
    lax.fori_loop(0, 2, compact, 0)
    w_stage2(0)
    w_stage1(1)
    wo_from_partner()
    states_of(0, 0)
    within_of(0, 0)
    w_stage3(0)

    ag_near(1)
    ag_far(1)
    row_scale(1)
    project_control(1)
    project_values(0, 1)
    lax.fori_loop(2, 4, compact, 0)
    hear(2)
    tot_sc[CHUNKS] = tot_sc[0] + tot_sc[1] + tot_sc[2] + tot_sc[3]
    log_recv[seq] = tot_sc[CHUNKS]

    def log_copy(k):
        peer = (seq + k) % NSEQ
        return remote(
            tot_sc.at[CHUNKS], log_recv.at[seq], s0_send.at[k], s0_recv.at[k], {"seq": peer}
        )

    def send_log(k, carry_):
        log_copy(k).start()
        return carry_

    lax.fori_loop(1, NSEQ, send_log, 0)

    states_of(0, 2)
    leave(0)
    w_finish(0)
    project_values(1, 0)
    w_stage2(1)
    project_values(1, 1)
    states_of(1, 0)
    states_of(1, 2)
    leave(1)

    def await_log(k, carry_):
        src = (seq + NSEQ - k) % NSEQ
        remote(
            tot_sc.at[CHUNKS], log_recv.at[src], s0_send.at[k], s0_recv.at[k], {"seq": src}
        ).wait_recv()
        return carry_

    def scan_devices(blk):
        def await_state(k, carry_):
            src = (seq + NSEQ - k) % NSEQ
            remote(
                st_send.at[blk, src], st_recv.at[blk, src], s1_send.at[blk, k], s1_recv.at[blk, k], {"seq": src}
            ).wait_recv()
            return carry_

        lax.fori_loop(1, NSEQ, await_state, 0)
        lanes = slice(blk * COLS, (blk + 1) * COLS)
        now = jnp.zeros((GROUP, COLS), F32)
        for d in range(NSEQ):
            enter[d, blk] = now
            if d < NSEQ - 1:
                begin = d * ROWS
                kept = keep_x[d, :, lanes] * keep_f(begin, begin + ROWS - 1)
                now = st_recv[blk, d].astype(F32)[0:GROUP] + kept * now
        now = jnp.zeros((GROUP, COLS), F32)
        for d in range(NSEQ - 1, -1, -1):
            en_send[blk, d] = jnp.concatenate([enter[d, blk], now], axis=0).astype(BF16)
            if d > 0:
                begin = d * ROWS
                kept = keep_x[d, :, lanes] * keep_b(begin, begin + ROWS - 1)
                now = st_recv[blk, d].astype(F32)[GROUP : 2 * GROUP] + kept * now

        def send_enter(k, carry_):
            enter_copy(blk, k).start()
            return carry_

        lax.fori_loop(1, NSEQ, send_enter, 0)
        en_recv[blk, seq] = en_send[blk, seq]

    def enter_copy(blk, k):
        peer = (seq + k) % NSEQ
        return remote(
            en_send.at[blk, peer], en_recv.at[blk, seq], s2_send.at[blk, k], s2_recv.at[blk, k], {"seq": peer}
        )

    lax.fori_loop(1, NSEQ, await_log, 0)
    keep_x[...] = jnp.exp2(exact(log_recv[...].reshape(NSEQ * 8, 128), spread)).reshape(NSEQ, 8, 2 * COLS)
    scan_devices(0)
    w_stage3(1)
    within_of(0, 2)
    g_copy.wait()
    project_gates(0)
    scan_devices(1)
    within_of(1, 0)
    within_of(1, 2)
    w_finish(1)
    project_gates(1)
    wo_to_twin()

    def outside(blk):
        def await_enter(k, carry_):
            src = (seq + NSEQ - k) % NSEQ
            remote(
                en_send.at[blk, src], en_recv.at[blk, src], s2_send.at[blk, k], s2_recv.at[blk, k], {"seq": src}
            ).wait_recv()
            return carry_

        lax.fori_loop(1, NSEQ, await_enter, 0)
        both = en_recv[blk].astype(F32)
        f = both[:, 0:GROUP].reshape(STATE, COLS)
        b = both[:, GROUP : 2 * GROUP].reshape(STATE, COLS)
        for c in range(CHUNKS):
            begin = base + c * CHUNK
            inner[blk, c, 0] = f.astype(BF16)
            if c < CHUNKS - 1:
                f = chunk_state[blk * CHUNKS + c, :, 0:COLS] + (
                    totx[blk, c, 0:1, :] * keep_f(begin, begin + CHUNK - 1)
                ) * f
        for c in range(CHUNKS - 1, -1, -1):
            begin = base + c * CHUNK
            inner[blk, c, 1] = b.astype(BF16)
            if c > 0:
                b = chunk_state[blk * CHUNKS + c, :, COLS:] + (
                    totx[blk, c, 0:1, :] * keep_b(begin, begin + CHUNK - 1)
                ) * b

    outside(0)
    outside(1)

    ones = jnp.ones((8, COLS), BF16)
    row8 = iota((8, CHUNK), 0)

    def gate(c, carry_):
        rows = pl.ds(pl.multiple_of(c * CHUNK, CHUNK), CHUNK)
        sums = jnp.zeros((8, CHUNK), F32)
        cc = c_sc[rows, STATE : 2 * STATE]
        for blk in range(2):
            a = act[blk, rows, :]
            for d, y in enumerate((y_f, y_b)):
                added = dot(cc, inner[blk, c, d]) * reach[blk, d, rows, :].astype(F32)
                v = (y[blk, rows, :] + added) * a
                y[blk, rows, :] = v
                sq = v * v
                hi = sq.astype(BF16)
                lo = (sq - hi.astype(F32)).astype(BF16)
                sums = sums + jnp.where(row8 == d, dot_nt(ones, hi) + dot_nt(ones, lo), 0.0)
        ps_mine[c // 2, :, pl.ds(pl.multiple_of((c % 2) * CHUNK, CHUNK), CHUNK)] = sums
        return carry_

    def send_sums(half):
        for k, device in enumerate((to_d, to_n, to_o)):
            send(ps_mine.at[half], ps_buf.at[half, k], ps_send.at[half, k], ps_recv.at[half, k], device)

    def norm_half(half):
        for k in range(3):
            remote(
                ps_mine.at[half], ps_buf.at[half, k], ps_send.at[half, k], ps_recv.at[half, k], to_n
            ).wait_recv()
        sums = ps_mine[half] + ps_buf[half, 0] + ps_buf[half, 1] + ps_buf[half, 2]
        scale = lax.rsqrt(sums * (1.0 / (COLS * NCHAN)) + norm_eps)
        scale = jnp.concatenate([scale, jnp.zeros((CHUNK - 8, HALF_ROWS), F32)], axis=0)
        for i in range(2):
            c = 2 * half + i
            rows = slice(c * CHUNK, (c + 1) * CHUNK)
            r = scale[:, i * CHUNK : (i + 1) * CHUNK].T
            for blk in range(2):
                both = y_f[blk, rows, :] * r[:, 0:1] + y_b[blk, rows, :] * r[:, 1:2]
                comb[rows, blk * COLS : (blk + 1) * COLS] = (both * gg[blk]).astype(BF16)

    lax.fori_loop(0, 2, gate, 0)
    send_sums(0)
    lax.fori_loop(2, 4, gate, 0)
    send_sums(1)
    wo_finish()
    o_copy.wait()
    remote(ggain_ref, gg.at[1], ag_send.at[0, 6], ag_recv.at[0, 6], to_w).wait_recv()

    def out_block(k, half):
        lanes = pl.ds(pl.multiple_of(k * COLS, COLS), COLS)
        rows = pl.ds(half * HALF_ROWS, HALF_ROWS)
        part[k, rows, :] = dot(comb[rows, :], wo[:, lanes]).astype(BF16)

    def quarter(half, i):
        return pl.ds((2 * half + i) * CHUNK, CHUNK)

    def rs(half, kind, src, dst, device):
        send(src, dst, rs_send.at[half, kind], rs_recv.at[half, kind], device)

    def rs_wait(half, kind, dst):
        remote(
            part.at[k_me, quarter(0, 0)], dst, rs_send.at[half, kind], rs_recv.at[half, kind], to_n
        ).wait_recv()

    def add(block, rows, ref):
        part[block, rows, :] = (part[block, rows, :].astype(F32) + ref[...].astype(F32)).astype(BF16)

    def produce(half):
        q1, q2 = quarter(half, 0), quarter(half, 1)
        out_block(k_d, half)
        rs(half, 0, part.at[k_d, q1], relay.at[half, 0], to_o)
        rs(half, 1, part.at[k_d, q2], relay.at[half, 1], to_n)
        out_block(k_n, half)
        rs(half, 2, part.at[k_n, q2], rs_buf.at[0, q2], to_n)
        out_block(k_o, half)
        rs(half, 4, part.at[k_o, q1], rs_buf.at[1, q1], to_o)

    def hand_on(half):
        q1, q2 = quarter(half, 0), quarter(half, 1)
        rs_wait(half, 0, relay.at[half, 0])
        add(k_n, q1, relay.at[half, 0])
        rs(half, 3, part.at[k_n, q1], rs_buf.at[0, q1], to_n)
        rs_wait(half, 1, relay.at[half, 1])
        add(k_o, q2, relay.at[half, 1])
        rs(half, 5, part.at[k_o, q2], rs_buf.at[1, q2], to_o)

    def finish(half):
        q1, q2 = quarter(half, 0), quarter(half, 1)
        rs_wait(half, 4, rs_buf.at[1, q1])
        rs_wait(half, 2, rs_buf.at[0, q2])
        rs_wait(half, 3, rs_buf.at[0, q1])
        rs_wait(half, 5, rs_buf.at[1, q2])
        rows = pl.ds(half * HALF_ROWS, HALF_ROWS)
        total = part[k_me, rows, :].astype(F32) + rs_buf[0, rows, :].astype(F32) + rs_buf[1, rows, :].astype(F32)
        out_ref[rows, :] = dot(total.astype(BF16), flip).astype(BF16)

    norm_half(0)
    produce(0)
    norm_half(1)
    hand_on(0)
    produce(1)
    out_block(k_me, 0)
    out_block(k_me, 1)
    hand_on(1)
    finish(0)
    finish(1)

    for copy in started:
        copy.wait_send()

    def sent_seq(k, carry_):
        log_copy(k).wait_send()
        for blk in range(2):
            state_copy(blk, k).wait_send()
            enter_copy(blk, k).wait_send()
        return carry_

    lax.fori_loop(1, NSEQ, sent_seq, 0)


def local(
    hidden, norm_gain, w_values, w_gates, w_control, dt_bias, decay_total, skip_gain, gate_gain, w_out, doc_starts
):
    vmem = pl.BlockSpec(memory_space=pltpu.VMEM)
    hbm = pl.BlockSpec(memory_space=pl.ANY)
    smem = pl.BlockSpec(memory_space=pltpu.SMEM)
    dma = pltpu.SemaphoreType.DMA
    scratch = [
        pltpu.VMEM((ROWS, COLS), BF16),
        pltpu.VMEM((2, HALF, COLS), BF16),
        pltpu.VMEM((2, HALF, COLS), BF16),
        pltpu.VMEM((CTRL, HALF), BF16),
        pltpu.VMEM((2 * COLS, HALF), BF16),
        pltpu.VMEM((2, 1, COLS), F32),
        pltpu.VMEM((4, ROWS, COLS), BF16),
        pltpu.VMEM((ROWS, HALF), BF16),
        pltpu.VMEM((ROWS, 128), F32),
        pltpu.VMEM((ROWS, 128), F32),
        pltpu.VMEM((ROWS, CTRL), BF16),
        pltpu.VMEM((CHUNKS, 5 * CHUNK, 128), BF16),
        pltpu.VMEM((CHUNKS, CHUNK, CHUNK), F32),
        pltpu.VMEM((2, ROWS, 128), F32),
        pltpu.VMEM((2, ROWS, 128), F32),
        pltpu.VMEM((2, CHUNKS, 8, 128), F32),
        pltpu.VMEM((2, CHUNKS, 8, 128), F32),
        pltpu.VMEM((2, ROWS, COLS), BF16),
        pltpu.VMEM((2, ROWS, COLS), BF16),
        pltpu.VMEM((2, ROWS, COLS), F32),
        pltpu.VMEM((2, 2, ROWS, COLS), BF16),
        pltpu.VMEM((2 * CHUNKS, STATE, 2 * COLS), F32),
        pltpu.VMEM((CHUNKS + 1, 8, 128), F32),
        pltpu.VMEM((2, CHUNKS, 8, COLS), F32),
        pltpu.VMEM((NSEQ, 8, 128), F32),
        pltpu.VMEM((NSEQ, 8, 2 * COLS), F32),
        pltpu.VMEM((2, NSEQ, 2 * GROUP, COLS), BF16),
        pltpu.VMEM((2, NSEQ, 2 * GROUP, COLS), BF16),
        pltpu.VMEM((NSEQ, 2, GROUP, COLS), F32),
        pltpu.VMEM((2, NSEQ, 2 * GROUP, COLS), BF16),
        pltpu.VMEM((2, NSEQ, 2 * GROUP, COLS), BF16),
        pltpu.VMEM((2, CHUNKS, 2, STATE, COLS), BF16),
        pltpu.VMEM((2, ROWS, COLS), F32),
        pltpu.VMEM((2, ROWS, COLS), F32),
        pltpu.VMEM((2, 3, 8, HALF_ROWS), F32),
        pltpu.VMEM((2, 8, HALF_ROWS), F32),
        pltpu.VMEM((ROWS, 2 * COLS), BF16),
        pltpu.VMEM((4, ROWS, COLS), BF16),
        pltpu.VMEM((2, ROWS, COLS), BF16),
        pltpu.VMEM((2, 2, CHUNK, COLS), BF16),
        dma((5,)),
        pltpu.SemaphoreType.REGULAR((3,)),
        dma((2, 7)),
        dma((2, 7)),
        dma((3, 10)),
        dma((3, 10)),
        dma((NSEQ,)),
        dma((NSEQ,)),
        dma((2, NSEQ)),
        dma((2, NSEQ)),
        dma((2, NSEQ)),
        dma((2, NSEQ)),
        dma((2, 3)),
        dma((2, 3)),
        dma((2, 6)),
        dma((2, 6)),
    ]
    return pl.pallas_call(
        kernel,
        name="mixer",
        out_shape=jax.ShapeDtypeStruct((ROWS, COLS), BF16),
        in_specs=[hbm, vmem, hbm, hbm, hbm, vmem, vmem, vmem, vmem, hbm, smem],
        out_specs=vmem,
        scratch_shapes=scratch,
        compiler_params=pltpu.CompilerParams(
            collective_id=0, has_side_effects=True, vmem_limit_bytes=56 * 2**20
        ),
    )(
        hidden,
        norm_gain.reshape(4, 1, COLS),
        w_values,
        w_gates,
        w_control.T,
        dt_bias.reshape(1, HEADS),
        decay_total.reshape(1, HEADS),
        skip_gain.reshape(1, HEADS),
        gate_gain.reshape(1, COLS),
        w_out,
        doc_starts,
    )


def solution(mesh):
    in_specs = (
        P("seq", "chan"),
        P(),
        P(None, "chan"),
        P(None, "chan"),
        P(),
        P(),
        P(),
        P(),
        P("chan"),
        P("chan", None),
        P(),
    )
    return jax.shard_map(local, mesh=mesh, in_specs=in_specs, out_specs=P("seq", "chan"), check_vma=False)
```
